256 devices in a mesh: expert: 8 (over y_lo, x), fsdp: 32 (over y_hi, z, core).
Axes of the slice: x: 4, y: 4 (y_hi: 2, y_lo: 2; y = y_hi * 2 + y_lo), z: 8, core: 2. Of those that a mesh axis runs over, the one named last changes fastest.
Arguments:
- tokens: bfloat16 [1024, 3072], P('expert'), may hold values from -6 to 6
- assignment: int32 [1024, 2], P('expert'), may hold values from 0 to 7, all different within a row; in each aligned block of 128 rows (0 to 127, 128 to 255, ...) at most 48 rows name the same one
- route_weight: float32 [1024, 2], P('expert'), may hold values from 0.25 to 1
- cotangent: bfloat16 [1024, 3072], P('expert'), may hold values from -6 to 6
- w_gate: bfloat16 [8, 3072, 8192], P('expert', None, 'fsdp'), may hold values from -0.109375 to 0.109375
- w_up: bfloat16 [8, 3072, 8192], P('expert', None, 'fsdp'), may hold values from -0.109375 to 0.109375
- w_down: bfloat16 [8, 8192, 3072], P('expert', 'fsdp'), may hold values from -0.0625 to 0.0625
Outputs:
- moe_out: bfloat16 [1024, 3072], P('expert')
- grad_tokens: bfloat16 [1024, 3072], P('expert')
- grad_prob: float32 [1024, 2], P('expert')
- grad_gate: bfloat16 [8, 3072, 8192], P('expert', None, 'fsdp')
- grad_up: bfloat16 [8, 3072, 8192], P('expert', None, 'fsdp')
- grad_down: bfloat16 [8, 8192, 3072], P('expert', 'fsdp')
The draws below stay inside these ranges and needn't reach their ends.
Inputs may be any that keep to these rules, and one draw needn't show every extreme that they name: `assignment`: each token names two different experts. Among the 128 tokens of one block no expert is named more than 48 times, and in some block some expert is named exactly 48 times.
All inputs are finite; a program needn't handle non-finite values.
Results may differ from the reference program's by a relative error of at most 0.02.
Values may be sent and summed in bfloat16 or wider, within the bound.
A program may use at most 128 MiB of HBM per device.

```python
import math
import jax
import jax.numpy as jnp
import numpy as np
from jax import lax

D = 3072
FF = 8192
TOK_DEV = 128
E = 8
CAP = 48
TOKENS = 1024
N_FSDP = 32


def level_of(stream_key, extent, shards, smallest, high):
    level = 1.0
    for dim, blocks in shards:
        draws = jax.random.uniform(jax.random.fold_in(jax.random.fold_in(stream_key, 6), dim), (blocks,), jnp.float32, smallest / len(shards), high / len(shards))
        level = level * jnp.repeat(jnp.exp(draws), extent[dim] // blocks).reshape((-1,) + (1,) * (len(extent) - 1 - dim))
    return level


def deal_out(stream_key, own, number, rows, count, top, most, skew):
    order = jax.random.permutation(stream_key, count)
    crowded, usual = load_shares(count, rows * top, most, skew, True), load_shares(count, rows * top, most, skew, False)
    places = jnp.arange(count)

    def named(tallies, turn):
        used = int((tallies > 0).sum())
        fixed = max(1, used // 4)
        moved = fixed + (places - fixed + turn * (used - fixed)) % max(1, count - fixed)
        return jnp.zeros((count,), jnp.int32).at[order[jnp.where(places < fixed, places, moved)]].set(jnp.asarray(tallies, jnp.int32))

    tallies = jnp.where(number % 4 == 0, named(crowded, number // 4), named(usual, number - number // 4 - 1))
    mixed = jax.random.permutation(jax.random.fold_in(own, 3), count)
    giver, taker = mixed[0:count // 2 * 2:2], mixed[1:count // 2 * 2:2]
    room = jnp.minimum(tallies[giver] - 1, most - tallies[taker]) // 2
    room = jnp.where((giver == order[0]) | (taker == order[0]) | (tallies[taker] == 0), 0, jnp.maximum(room, 0))
    moved = jax.random.randint(jax.random.fold_in(own, 4), (count // 2,), 0, 1 << 20) % (room + 1)
    tallies = tallies.at[giver].add(-moved).at[taker].add(moved)
    members = jnp.searchsorted(jnp.cumsum(tallies), jnp.arange(rows * top), side="right").astype(jnp.int32)
    grid = members.reshape(top, rows).T
    grid = grid[jax.random.permutation(jax.random.fold_in(own, 1), rows)]
    turn = jax.random.randint(jax.random.fold_in(own, 2), (rows, 1), 0, top)
    return jnp.take_along_axis(grid, (jnp.arange(top)[None, :] + turn) % top, axis=1)


def load_shares(amount, total, most, skew, full):
    portions = [(1 << 20) // math.isqrt(grade ** skew) + 1 for grade in range(1, amount + 1)]
    largest = most if full else min(most, max(-(-total // amount), total * portions[0] // sum(portions)))
    least = 1 if total - largest >= amount - 1 else 0
    holding, spare = [largest] + [least] * (amount - 1), total - largest - least * (amount - 1)
    while spare > 0:
        free = [i for i in range(1, amount) if holding[i] < largest] or [i for i in range(1, amount) if holding[i] < most]
        whole, remaining = sum([portions[i] for i in free]), spare
        for i in free:
            addition = min(most - holding[i], max(1, remaining * portions[i] // whole), spare)
            holding[i] = holding[i] + addition
            spare = spare - addition
    return np.array(holding)


def bell_draw(own_key, shape, scale, most, pieces=(), held_as=jnp.bfloat16):
    level = level_of(own_key, shape, pieces, -0.22, 0.18) if pieces else 1.0
    values = jax.random.normal(own_key, shape, jnp.float32) * scale * level
    return jnp.minimum(jnp.maximum(values, -most), most).astype(held_as)


def setup_inputs(seed: int = 0) -> dict:
    streams_of = jax.random.split(jax.random.key(seed), 8)
    tokens = bell_draw(streams_of[0], (TOKENS, D), 1.0, 6.0, ((0, 8),))
    assignment_keys = jax.random.split(jax.random.fold_in(streams_of[1], 1), TOKENS // TOK_DEV)
    assignment_turns = jax.random.permutation(jax.random.fold_in(streams_of[1], 3), TOKENS // TOK_DEV)
    assignment = jax.vmap(lambda own, number: deal_out(jax.random.fold_in(streams_of[1], 2), own, number, TOK_DEV, E, 2, CAP, 2))(assignment_keys, assignment_turns).reshape((TOKENS, 2))
    route_weight = jnp.clip(0.25 + 0.75 * jax.random.uniform(streams_of[2], (TOKENS, 2), jnp.float32) ** level_of(streams_of[2], (TOKENS, 2), ((0, 8),), -0.2, 0.2), 0.25, 1.0)
    cotangent = bell_draw(streams_of[3], (TOKENS, D), 1.0, 6.0, ((0, 8),))
    w_gate = bell_draw(streams_of[4], (E, D, FF), D ** -0.5, 0.109375, ((0, 8), (2, 32)))
    w_up = bell_draw(streams_of[5], (E, D, FF), D ** -0.5, 0.109375, ((0, 8), (2, 32)))
    w_down = bell_draw(streams_of[6], (E, FF, D), FF ** -0.5, 0.0625, ((0, 8), (1, 32)))
    return dict(tokens=tokens, assignment=assignment, route_weight=route_weight, cotangent=cotangent, w_gate=w_gate, w_up=w_up, w_down=w_down)


def slot_table(assignment):
    flat = assignment.reshape(-1)
    onehot = (flat[:, None] == jnp.arange(E, dtype=jnp.int32)[None, :]).astype(jnp.int32)
    before = jnp.cumsum(onehot, axis=0) - onehot
    position = jnp.sum(before * onehot, axis=1).astype(jnp.int32)
    return (flat * CAP + position).astype(jnp.int32).reshape(assignment.shape)


def rounded(value):
    return lax.optimization_barrier(value.astype(jnp.bfloat16)).astype(jnp.float32)


def piece_sums(term, rows):
    def step(total, index):
        return total + rounded(term(index)), None

    start = jnp.zeros((rows, D), jnp.float32)
    total, _ = lax.scan(step, start, jnp.arange(N_FSDP, dtype=jnp.int32))
    return total.astype(jnp.bfloat16)


def expert_pass(rows_x, rows_dy, gate_mat, up_mat, down_mat):
    piece = FF // N_FSDP
    rows = rows_x.shape[0]
    pre_gate = jnp.dot(rows_x, gate_mat, preferred_element_type=jnp.float32)
    pre_up = jnp.dot(rows_x, up_mat, preferred_element_type=jnp.float32)
    sigma = jax.nn.sigmoid(pre_gate)
    silu_gate = pre_gate * sigma
    hidden = (silu_gate * pre_up).astype(jnp.bfloat16)

    def out_term(index):
        part = lax.dynamic_slice_in_dim(hidden, index * piece, piece, 1)
        down_part = lax.dynamic_slice_in_dim(down_mat, index * piece, piece, 0)
        return jnp.dot(part, down_part, preferred_element_type=jnp.float32)

    expert_out = piece_sums(out_term, rows)
    grad_hidden = jnp.dot(rows_dy, down_mat.T, preferred_element_type=jnp.float32)
    grad_down = jnp.dot(hidden.T, rows_dy, preferred_element_type=jnp.float32).astype(jnp.bfloat16)
    grad_pre_gate = (grad_hidden * pre_up * sigma * (1.0 + pre_gate * (1.0 - sigma))).astype(jnp.bfloat16)
    grad_pre_up = (grad_hidden * silu_gate).astype(jnp.bfloat16)
    grad_gate = jnp.dot(rows_x.T, grad_pre_gate, preferred_element_type=jnp.float32).astype(jnp.bfloat16)
    grad_up = jnp.dot(rows_x.T, grad_pre_up, preferred_element_type=jnp.float32).astype(jnp.bfloat16)

    def back_term(index):
        gate_part = lax.dynamic_slice_in_dim(grad_pre_gate, index * piece, piece, 1)
        up_part = lax.dynamic_slice_in_dim(grad_pre_up, index * piece, piece, 1)
        gate_cols = lax.dynamic_slice_in_dim(gate_mat, index * piece, piece, 1)
        up_cols = lax.dynamic_slice_in_dim(up_mat, index * piece, piece, 1)
        return (jnp.dot(gate_part, gate_cols.T, preferred_element_type=jnp.float32)
                + jnp.dot(up_part, up_cols.T, preferred_element_type=jnp.float32))

    slot_grad = piece_sums(back_term, rows)
    return expert_out, slot_grad, grad_gate, grad_up, grad_down


def reference(tokens, assignment, route_weight, cotangent, w_gate, w_up, w_down):
    blocks = TOKENS // TOK_DEV
    slot_count = E * CAP
    table = jax.vmap(slot_table)(assignment.reshape(blocks, TOK_DEV, 2))
    block_ids = jnp.broadcast_to(jnp.arange(blocks, dtype=jnp.int32)[:, None, None], table.shape)
    rows_in = jnp.broadcast_to(tokens.reshape(blocks, TOK_DEV, 1, D), (blocks, TOK_DEV, 2, D))
    sent_tokens = jnp.zeros((blocks, slot_count, D), jnp.bfloat16).at[block_ids, table].set(rows_in)
    weights3 = route_weight.reshape(blocks, TOK_DEV, 2)
    cot_f = cotangent.reshape(blocks, TOK_DEV, 1, D).astype(jnp.float32)
    weighted = (weights3[..., None] * cot_f).astype(jnp.bfloat16)
    sent_cot = jnp.zeros((blocks, slot_count, D), jnp.bfloat16).at[block_ids, table].set(weighted)
    out_list, grad_list, gate_list, up_list, down_list = [], [], [], [], []
    for expert in range(E):
        rows_x = sent_tokens[:, expert * CAP:(expert + 1) * CAP].reshape(-1, D)
        rows_dy = sent_cot[:, expert * CAP:(expert + 1) * CAP].reshape(-1, D)
        result = expert_pass(rows_x, rows_dy, w_gate[expert], w_up[expert], w_down[expert])
        out_list.append(result[0].reshape(blocks, CAP, D))
        grad_list.append(result[1].reshape(blocks, CAP, D))
        gate_list.append(result[2])
        up_list.append(result[3])
        down_list.append(result[4])
    out_slots = jnp.concatenate(out_list, axis=1)
    grad_slots = jnp.concatenate(grad_list, axis=1)
    route_out = out_slots[block_ids, table].astype(jnp.float32)
    route_grad = grad_slots[block_ids, table].astype(jnp.float32)
    moe_out = jnp.sum(weights3[..., None] * route_out, axis=2).astype(jnp.bfloat16).reshape(TOKENS, D)
    grad_prob = jnp.sum(cot_f * route_out, axis=3).reshape(TOKENS, 2)
    grad_tokens = jnp.sum(route_grad, axis=2).astype(jnp.bfloat16).reshape(TOKENS, D)
    return (moe_out, grad_tokens, grad_prob, jnp.stack(gate_list), jnp.stack(up_list), jnp.stack(down_list))
```

```python
import functools

import jax
import jax.numpy as jnp
from jax import lax
from jax.experimental import pallas as pl
from jax.experimental.pallas import tpu as pltpu
from jax.sharding import PartitionSpec as P

MESH = pl.DeviceIdType.MESH
BF16 = jnp.bfloat16
F32 = jnp.float32
NT = (((1,), (1,)), ((), ()))
TN = (((0,), (0,)), ((), ()))

E = 8
NZ = 8
CAP = 48
TOK = 128
SLOTS = E * CAP
D = 3072
H = 256
HALF = SLOTS // 2
KS = 256
NK = D // KS
ND = NK - NZ
RS = D // NZ


def rows_of(index, size):
    return pl.ds(pl.multiple_of(index * size, size), size)


def kernel(
    tokens, assignment, weight, cotangent, w_gate, w_up, w_down,
    moe_out, grad_tokens, grad_prob, grad_gate, grad_up, grad_down,
    acts, cot_part, wgu, wd, send_s, send_d, xd, acc_gu, acc_h, hid, gpre,
    part, rp, rm, rc, gp, outs, gg, gu, gd,
    load_sem, wpre_sem, store_sem,
    a_send, a_recv, d_send, d_recv, ring_send, ring_recv, sib_send, sib_recv, dsib_sem,
    act_sem, rs_send, rs_recv, c_send, c_recv, o_send, o_recv, osib_send, osib_recv, g_send, g_recv,
):
    e = lax.axis_index("expert")
    f = lax.axis_index("fsdp")
    core = lax.rem(f, 2)
    z = lax.rem(lax.div(f, 2), NZ)
    yh = lax.div(f, 2 * NZ)
    t = core

    def dev(e_, yh_, z_, c_):
        return (e_, yh_ * (2 * NZ) + z_ * 2 + c_)

    sibling = dev(e, yh, z, 1 - core)
    up = dev(e, yh, lax.rem(z + 1, NZ), core)
    down = dev(e, yh, lax.rem(z + NZ - 1, NZ), core)

    def zmod(v):
        return lax.rem(v + 2 * NZ, NZ)

    pending = []

    def remote(src, dst, ss, rs, device):
        return pltpu.make_async_remote_copy(
            src_ref=src, dst_ref=dst, send_sem=ss, recv_sem=rs, device_id=device, device_id_type=MESH
        )

    def send(src, dst, ss, rs, device):
        c = remote(src, dst, ss, rs, device)
        c.start()
        pending.append(c)

    def arrived(dst, ss, rs):
        remote(dst, dst, ss, rs, sibling).wait_recv()

    load_x = pltpu.make_async_copy(tokens, acts, load_sem.at[0])
    load_y = pltpu.make_async_copy(cotangent, acts, load_sem.at[0])

    @pl.when(core == 0)
    def _():
        load_x.start()

    @pl.when(core == 1)
    def _():
        load_y.start()

    own_g = pltpu.make_async_copy(w_gate.at[0], wgu.at[:, rows_of(core, H)], load_sem.at[1])
    own_u = pltpu.make_async_copy(w_up.at[0], wgu.at[:, rows_of(core + 2, H)], load_sem.at[2])
    own_d = pltpu.make_async_copy(w_down.at[0], wd.at[rows_of(core, H), :], load_sem.at[3])
    own_c = pltpu.make_async_copy(cotangent.at[:, rows_of(z, RS)], cot_part, load_sem.at[4])
    for c in (own_g, own_u, own_d, own_c):
        c.start()

    barrier = pltpu.get_barrier_semaphore()

    def greet(device):
        pl.semaphore_signal(barrier, inc=1, device_id=device, device_id_type=MESH)

    for i in range(E):
        for dy in range(2):
            if i or dy:
                greet(dev(lax.rem(e + i, E), lax.rem(yh + dy, 2), z, core))
    for dz in range(NZ):
        for dc in range(2):
            if dz or dc:
                greet(dev(e, yh, lax.rem(z + dz, NZ), lax.rem(core + dc, 2)))

    a = assignment[...]
    rw = weight[...]
    lane = lax.broadcasted_iota(jnp.int32, (TOK, TOK), 1)
    row = lax.broadcasted_iota(jnp.int32, (TOK, TOK), 0)
    hot0 = (a[:, 0:1] == lane).astype(F32)
    hot1 = (a[:, 1:2] == lane).astype(F32)
    below = (row > lane).astype(BF16)
    count = jnp.dot(below, (hot0 + hot1).astype(BF16), preferred_element_type=F32)
    pos0 = jnp.sum(hot0 * count, axis=1, keepdims=True)
    pos1 = jnp.sum(hot1 * count, axis=1, keepdims=True)
    slot0 = a[:, 0:1] * CAP + pos0.astype(jnp.int32)
    slot1 = a[:, 1:2] * CAP + pos1.astype(jnp.int32)
    slot_lane = lax.broadcasted_iota(jnp.int32, (TOK, SLOTS), 1)
    pick0 = (slot0 == slot_lane).astype(F32)
    pick1 = (slot1 == slot_lane).astype(F32)
    spread = jnp.concatenate([pick0.T, pick1.T], axis=1).astype(BF16)
    w0 = rw[:, 0:1]
    w1 = rw[:, 1:2]
    is_x = core == 0
    in0 = jnp.where(is_x, 1.0, w0)
    in1 = jnp.where(is_x, 1.0, w1)

    def dispatch(cols):
        v = cols.astype(F32)
        both = jnp.concatenate([(in0 * v).astype(BF16), (in1 * v).astype(BF16)], axis=0)
        return jnp.dot(spread, both, preferred_element_type=F32).astype(BF16)

    @pl.when(core == 0)
    def _():
        load_x.wait()

    @pl.when(core == 1)
    def _():
        load_y.wait()

    send_s[...] = dispatch(acts[:, rows_of(z, KS)])
    own_rows = rows_of(e, CAP)
    xd[t, z, own_rows, :] = send_s[own_rows, :]

    pl.semaphore_wait(barrier, 2 * E - 1 + 2 * NZ - 1)

    for i in range(1, E):
        j = lax.rem(e + i, E)
        send(
            send_s.at[rows_of(j, CAP), :], xd.at[t, z, own_rows, :],
            a_send.at[i - 1], a_recv.at[i - 1], dev(j, yh, z, core),
        )

    @pl.when(core == 0)
    def _():
        remote(w_gate.at[0], wgu.at[:, 0:H], wpre_sem.at[0], wpre_sem.at[2], sibling).start()
        remote(w_up.at[0], wgu.at[:, 2 * H : 3 * H], wpre_sem.at[1], wpre_sem.at[3], sibling).start()

    @pl.when(core == 1)
    def _():
        remote(w_down.at[0], wd.at[H : 2 * H, :], wpre_sem.at[0], wpre_sem.at[2], sibling).start()

    for k in range(ND):
        send_d[k] = dispatch(acts[:, (NZ + k) * KS : (NZ + k + 1) * KS])
    for k in range(ND):
        xd[t, NZ + k, own_rows, :] = send_d[k, own_rows, :]
    for i in range(1, E):
        j = lax.rem(e + i, E)
        send(
            send_d.at[:, rows_of(j, CAP), :], xd.at[t, NZ:NK, own_rows, :],
            d_send.at[i - 1], d_recv.at[i - 1], dev(j, yh, z, core),
        )

    def gather(view, sems, slot, after_step):
        s_send, s_recv, b_send, b_recv = sems

        def pass_on(d, h):
            ref = view(slot, zmod(z + d), h)
            send(ref, ref, b_send.at[d % NZ, h], b_recv.at[d % NZ, h], sibling)

        for s in range(5):
            for h in range(2):
                for way, nxt, sign in ((0, up, -1), (1, down, 1)):
                    full = s < 4 or h == way
                    if not full:
                        continue
                    ref = view(slot, zmod(z + sign * s), h)
                    if s > 0:
                        arrived(ref, s_send.at[way, s - 1, h], s_recv.at[way, s - 1, h])
                    if s < 3 or (s == 3 and h == way):
                        send(ref, ref, s_send.at[way, s, h], s_recv.at[way, s, h], nxt)
                    if s > 0 or way == 0:
                        pass_on(sign * s, h)
            after_step(s)

    def xd_view(slot, zz, h):
        return xd.at[slot, zz, h * HALF : (h + 1) * HALF, :]

    for i in range(1, E):
        src = rows_of(lax.rem(e + E - i, E), CAP)
        arrived(xd.at[t, z, src, :], a_send.at[i - 1], a_recv.at[i - 1])

    def nothing(s):
        pass

    gather(xd_view, (ring_send, ring_recv, sib_send, sib_recv), t, nothing)

    for i in range(1, E):
        src = rows_of(lax.rem(e + E - i, E), CAP)
        arrived(xd.at[t, NZ:NK, src, :], d_send.at[i - 1], d_recv.at[i - 1])
    send(xd.at[t, NZ:NK], xd.at[t, NZ:NK], dsib_sem.at[0], dsib_sem.at[1], sibling)
    other = 1 - t
    for d in range(NZ):
        for h in range(2):
            arrived(xd_view(other, zmod(z + d), h), sib_send.at[d, h], sib_recv.at[d, h])
    arrived(xd.at[other, NZ:NK], dsib_sem.at[0], dsib_sem.at[1])
    for c in (own_g, own_u, own_d, own_c):
        c.wait()

    mine_g = rows_of(core, H)
    mine_u = rows_of(core + 2, H)
    acc_gu[...] = jnp.zeros_like(acc_gu)
    acc_h[...] = jnp.zeros_like(acc_h)

    @pl.loop(0, NK)
    def _(k):
        kr = rows_of(k, KS)
        acc_gu[:, 0:H] += jnp.dot(xd[0, k], wgu[kr, mine_g], preferred_element_type=F32)
        acc_gu[:, H : 2 * H] += jnp.dot(xd[0, k], wgu[kr, mine_u], preferred_element_type=F32)
        acc_h[...] += lax.dot_general(xd[1, k], wd[mine_g, kr], NT, preferred_element_type=F32)

    @pl.loop(0, E)
    def _(b):
        r = rows_of(b, CAP)
        pre_gate = acc_gu[r, 0:H]
        pre_up = acc_gu[r, H : 2 * H]
        grad_hidden = acc_h[r, :]
        sigma = jax.nn.sigmoid(pre_gate)
        silu = pre_gate * sigma
        hid[r, mine_g] = (silu * pre_up).astype(BF16)
        gpre[r, mine_g] = (grad_hidden * pre_up * sigma * (1.0 + pre_gate * (1.0 - sigma))).astype(BF16)
        gpre[r, mine_u] = (grad_hidden * silu).astype(BF16)

    @pl.when(core == 0)
    def _():
        cg = remote(gpre.at[:, 0:H], gpre.at[:, 0:H], act_sem.at[0], act_sem.at[2], sibling)
        cu = remote(gpre.at[:, 2 * H : 3 * H], gpre.at[:, 2 * H : 3 * H], act_sem.at[1], act_sem.at[3], sibling)
        cg.start()
        cu.start()
        arrived(wd.at[H : 2 * H, :], wpre_sem.at[0], wpre_sem.at[2])
        arrived(hid.at[:, H : 2 * H], act_sem.at[0], act_sem.at[2])

    @pl.when(core == 1)
    def _():
        ch = remote(hid.at[:, H : 2 * H], hid.at[:, H : 2 * H], act_sem.at[0], act_sem.at[2], sibling)
        ch.start()
        arrived(wgu.at[:, 0:H], wpre_sem.at[0], wpre_sem.at[2])
        arrived(wgu.at[:, 2 * H : 3 * H], wpre_sem.at[1], wpre_sem.at[3])
        arrived(gpre.at[:, 0:H], act_sem.at[0], act_sem.at[2])
        arrived(gpre.at[:, 2 * H : 3 * H], act_sem.at[1], act_sem.at[3])

    def term(zd):
        cols = rows_of(zd, RS)

        @pl.when(core == 0)
        def _():
            part[zd] = jnp.dot(hid[...], wd[:, cols], preferred_element_type=F32).astype(BF16)

        @pl.when(core == 1)
        def _():
            part[zd] = lax.dot_general(gpre[...], wgu[cols, :], NT, preferred_element_type=F32).astype(BF16)

    land = (rp, rm)

    def half(h):
        return slice(h * HALF, (h + 1) * HALF)

    def target(way, s):
        return zmod(z + 4 - s) if way == 0 else zmod(z - 4 + s)

    def rs_start(way, s, h):
        send(
            part.at[target(way, s), half(h), :], land[way].at[s, half(h), :],
            rs_send.at[way, s, h], rs_recv.at[way, s, h], up if way == 0 else down,
        )

    def rs_arrived(way, s, h):
        arrived(land[way].at[s, half(h), :], rs_send.at[way, s, h], rs_recv.at[way, s, h])

    def rs_add(way, s, h):
        zd = target(way, s + 1)
        part[zd, half(h), :] = (
            part[zd, half(h), :].astype(F32) + land[way][s, half(h), :].astype(F32)
        ).astype(BF16)

    term(zmod(z + 4))
    rs_start(0, 0, 0)
    rs_start(1, 0, 1)
    term(zmod(z + 3))
    rs_start(0, 1, 1)
    term(zmod(z + 5))
    rs_start(1, 1, 0)

    @pl.loop(0, 5)
    def _(i):
        term(zmod(z + 6 + i))

    @pl.loop(0, NK)
    def _(k):
        kr = rows_of(k, KS)
        g = lax.dot_general(xd[0, k], gpre[:, mine_g], TN, preferred_element_type=F32)
        gg[kr, :] = g.astype(BF16)
        u = lax.dot_general(xd[0, k], gpre[:, mine_u], TN, preferred_element_type=F32)
        gu[kr, :] = u.astype(BF16)
        w = lax.dot_general(hid[:, mine_g], xd[1, k], TN, preferred_element_type=F32)
        gd[:, kr] = w.astype(BF16)

    store_g = pltpu.make_async_copy(gg, grad_gate.at[0], store_sem.at[0])
    store_u = pltpu.make_async_copy(gu, grad_up.at[0], store_sem.at[1])
    store_d = pltpu.make_async_copy(gd, grad_down.at[0], store_sem.at[2])
    for c in (store_g, store_u, store_d):
        c.start()

    for way, h in ((0, 0), (1, 1)):
        rs_arrived(way, 0, h)
        rs_add(way, 0, h)
        rs_start(way, 1, h)
    for s in (1, 2):
        for way, h in ((0, 1), (1, 0), (0, 0), (1, 1)):
            rs_arrived(way, s, h)
            rs_add(way, s, h)
            rs_start(way, s + 1, h)
    for h in range(2):
        for way in range(2):
            rs_arrived(way, 3, h)
        part[z, half(h), :] = (
            part[z, half(h), :].astype(F32)
            + rp[3, half(h), :].astype(F32)
            + rm[3, half(h), :].astype(F32)
        ).astype(BF16)

    rc[yh, own_rows, :] = part[z, own_rows, :]
    for i in range(E):
        for dy in range(2):
            if i or dy:
                b = lax.rem(e + i, E)
                send(
                    part.at[z, rows_of(b, CAP), :], rc.at[yh, own_rows, :],
                    c_send.at[i, dy], c_recv.at[i, dy], dev(b, lax.rem(yh + dy, 2), z, core),
                )
    for i in range(E):
        for dy in range(2):
            if i or dy:
                src = rows_of(lax.rem(e + E - i, E), CAP)
                arrived(rc.at[lax.rem(yh + dy, 2), src, :], c_send.at[i, dy], c_recv.at[i, dy])

    summed = (rc[0].astype(F32) + rc[1].astype(F32)).astype(BF16)
    out0 = jnp.dot(pick0.astype(BF16), summed, preferred_element_type=F32)
    out1 = jnp.dot(pick1.astype(BF16), summed, preferred_element_type=F32)
    on0 = jnp.where(is_x, w0, 1.0)
    on1 = jnp.where(is_x, w1, 1.0)
    outs[t, z] = (on0 * out0 + on1 * out1).astype(BF16)
    cot = cot_part[...].astype(F32)
    p0 = jnp.sum(cot * out0, axis=1, keepdims=True)
    p1 = jnp.sum(cot * out1, axis=1, keepdims=True)
    both = jnp.where(lane == 0, p0, 0.0) + jnp.where(lane == 1, p1, 0.0)

    @pl.when(core == 0)
    def _():
        gp[z] = both.T[0:8, :]
        for dz in range(NZ):
            for dc in range(2):
                if dz or dc:
                    remote(
                        gp.at[z], gp.at[z], g_send.at[dz, dc], g_recv.at[dz, dc],
                        dev(e, yh, lax.rem(z + dz, NZ), dc),
                    ).start()

    def out_view(slot, zz, h):
        return outs.at[slot, zz, h * (TOK // 2) : (h + 1) * (TOK // 2), :]

    gather(out_view, (o_send, o_recv, osib_send, osib_recv), t, nothing)

    for d in range(NZ):
        for h in range(2):
            arrived(out_view(other, zmod(z + d), h), osib_send.at[d, h], osib_recv.at[d, h])
    for zz in range(NZ):
        pltpu.make_async_copy(outs.at[0, zz], moe_out.at[:, zz * RS : (zz + 1) * RS], store_sem.at[3 + zz]).start()
        pltpu.make_async_copy(
            outs.at[1, zz], grad_tokens.at[:, zz * RS : (zz + 1) * RS], store_sem.at[3 + NZ + zz]
        ).start()

    @pl.when(core == 0)
    def _():
        for dz in range(1, NZ):
            src = zmod(z - dz)
            remote(gp.at[src], gp.at[src], g_send.at[dz, 0], g_recv.at[dz, 0], sibling).wait_recv()
        for dz in range(NZ):
            for dc in range(2):
                if dz or dc:
                    remote(gp.at[z], gp.at[z], g_send.at[dz, dc], g_recv.at[dz, dc], sibling).wait_send()

    @pl.when(core == 1)
    def _():
        for dz in range(NZ):
            src = zmod(z - dz)
            remote(gp.at[src], gp.at[src], g_send.at[dz, 1], g_recv.at[dz, 1], sibling).wait_recv()

    total = gp[0]
    for zz in range(1, NZ):
        total = total + gp[zz]
    grad_prob[...] = total

    for c in (store_g, store_u, store_d):
        c.wait()
    for zz in range(NZ):
        pltpu.make_async_copy(outs.at[0, zz], moe_out.at[:, zz * RS : (zz + 1) * RS], store_sem.at[3 + zz]).wait()
        pltpu.make_async_copy(
            outs.at[1, zz], grad_tokens.at[:, zz * RS : (zz + 1) * RS], store_sem.at[3 + NZ + zz]
        ).wait()
    for c in pending:
        c.wait_send()

    @pl.when(core == 0)
    def _():
        remote(w_gate.at[0], wgu.at[:, 0:H], wpre_sem.at[0], wpre_sem.at[2], sibling).wait_send()
        remote(w_up.at[0], wgu.at[:, 2 * H : 3 * H], wpre_sem.at[1], wpre_sem.at[3], sibling).wait_send()
        remote(gpre.at[:, 0:H], gpre.at[:, 0:H], act_sem.at[0], act_sem.at[2], sibling).wait_send()
        remote(gpre.at[:, 2 * H : 3 * H], gpre.at[:, 2 * H : 3 * H], act_sem.at[1], act_sem.at[3], sibling).wait_send()

    @pl.when(core == 1)
    def _():
        remote(w_down.at[0], wd.at[H : 2 * H, :], wpre_sem.at[0], wpre_sem.at[2], sibling).wait_send()
        remote(hid.at[:, H : 2 * H], hid.at[:, H : 2 * H], act_sem.at[0], act_sem.at[2], sibling).wait_send()


def per_device(tokens, assignment, route_weight, cotangent, w_gate, w_up, w_down):
    hbm = pl.BlockSpec(memory_space=pl.ANY)
    vmem = pl.BlockSpec(memory_space=pltpu.VMEM)
    dma = pltpu.SemaphoreType.DMA
    res = pl.pallas_call(
        kernel,
        out_shape=(
            jax.ShapeDtypeStruct((TOK, D), BF16),
            jax.ShapeDtypeStruct((TOK, D), BF16),
            jax.ShapeDtypeStruct((8, TOK), F32),
            jax.ShapeDtypeStruct((1, D, H), BF16),
            jax.ShapeDtypeStruct((1, D, H), BF16),
            jax.ShapeDtypeStruct((1, H, D), BF16),
        ),
        in_specs=[hbm, vmem, vmem, hbm, hbm, hbm, hbm],
        out_specs=(hbm, hbm, vmem, hbm, hbm, hbm),
        scratch_shapes=[
            pltpu.VMEM((TOK, D), BF16),
            pltpu.VMEM((TOK, RS), BF16),
            pltpu.VMEM((D, 4 * H), BF16),
            pltpu.VMEM((2 * H, D), BF16),
            pltpu.VMEM((SLOTS, KS), BF16),
            pltpu.VMEM((ND, SLOTS, KS), BF16),
            pltpu.VMEM((2, NK, SLOTS, KS), BF16),
            pltpu.VMEM((SLOTS, 2 * H), F32),
            pltpu.VMEM((SLOTS, H), F32),
            pltpu.VMEM((SLOTS, 2 * H), BF16),
            pltpu.VMEM((SLOTS, 4 * H), BF16),
            pltpu.VMEM((NZ, SLOTS, RS), BF16),
            pltpu.VMEM((4, SLOTS, RS), BF16),
            pltpu.VMEM((4, SLOTS, RS), BF16),
            pltpu.VMEM((2, SLOTS, RS), BF16),
            pltpu.VMEM((NZ, 8, TOK), F32),
            pltpu.VMEM((2, NZ, TOK, RS), BF16),
            pltpu.VMEM((D, H), BF16),
            pltpu.VMEM((D, H), BF16),
            pltpu.VMEM((H, D), BF16),
            dma((5,)), dma((4,)), dma((3 + 2 * NZ,)),
            dma((E - 1,)), dma((E - 1,)), dma((E - 1,)), dma((E - 1,)),
            dma((2, 4, 2)), dma((2, 4, 2)), dma((NZ, 2)), dma((NZ, 2)), dma((2,)),
            dma((4,)), dma((2, 4, 2)), dma((2, 4, 2)), dma((E, 2)), dma((E, 2)),
            dma((2, 4, 2)), dma((2, 4, 2)), dma((NZ, 2)), dma((NZ, 2)), dma((NZ, 2)), dma((NZ, 2)),
        ],
        compiler_params=pltpu.CompilerParams(
            collective_id=0, has_side_effects=True, vmem_limit_bytes=60 * 1024 * 1024
        ),
    )(tokens, assignment, route_weight, cotangent, w_gate, w_up, w_down)
    moe_out, grad_tokens, prob, grad_gate, grad_up, grad_down = res
    return (moe_out, grad_tokens, prob[0:2].T, grad_gate, grad_up, grad_down)


def solution(mesh):
    return jax.shard_map(
        per_device,
        mesh=mesh,
        in_specs=(
            P("expert", None),
            P("expert", None),
            P("expert", None),
            P("expert", None),
            P("expert", None, "fsdp"),
            P("expert", None, "fsdp"),
            P("expert", "fsdp", None),
        ),
        out_specs=(
            P("expert", None),
            P("expert", None),
            P("expert", None),
            P("expert", None, "fsdp"),
            P("expert", None, "fsdp"),
            P("expert", "fsdp", None),
        ),
        check_vma=False,
    )
```

```python
import jax
import jax.numpy as jnp
from jax import lax
from jax.experimental import pallas as pl
from jax.experimental.pallas import tpu as pltpu
from jax.sharding import PartitionSpec as P

MESH = pl.DeviceIdType.MESH
BF16 = jnp.bfloat16
F32 = jnp.float32
NT = (((1,), (1,)), ((), ()))
TN = (((0,), (0,)), ((), ()))

E = 8
NZ = 8
CAP = 48
TOK = 128
SLOTS = E * CAP
D = 3072
H = 256
HALF = SLOTS // 2
KS = 256
NK = D // KS
ND = NK - NZ
RS = D // NZ
QC = 128
NQ = RS // QC
NP = 4


def rows_of(index, size):
    return pl.ds(pl.multiple_of(index * size, size), size)


def kernel(
    tokens, assign_t, weight_t, cotangent, w_gate, w_up, w_down,
    outs, prob, gg, gu, gd,
    acts_s, acts_d, cot_part, wgu, wd, send_s, send_d, xd, acc_gu, acc_h, hid, gpre,
    part, rp, rm, rc, gp,
    load_sem, wpre_sem,
    a_send, a_recv, d_send, d_recv, ring_send, ring_recv, sib_send, sib_recv, dsib_sem,
    act_sem, rs_send, rs_recv, c_send, c_recv, o_send, o_recv, osib_send, osib_recv, g_send, g_recv,
):
    e = lax.axis_index("expert")
    f = lax.axis_index("fsdp")
    core = lax.rem(f, 2)
    z = lax.rem(lax.div(f, 2), NZ)
    yh = lax.div(f, 2 * NZ)
    t = core
    other = 1 - core

    def dev(e_, yh_, z_, c_):
        return (e_, yh_ * (2 * NZ) + z_ * 2 + c_)

    sibling = dev(e, yh, z, 1 - core)
    up = dev(e, yh, lax.rem(z + 1, NZ), core)
    down = dev(e, yh, lax.rem(z + NZ - 1, NZ), core)

    def zmod(v):
        return lax.rem(v + 2 * NZ, NZ)

    pending = []

    def remote(src, dst, ss, rs, device):
        return pltpu.make_async_remote_copy(
            src_ref=src, dst_ref=dst, send_sem=ss, recv_sem=rs, device_id=device, device_id_type=MESH
        )

    def send(src, dst, ss, rs, device):
        c = remote(src, dst, ss, rs, device)
        c.start()
        pending.append(c)

    def arrived(dst, ss, rs):
        remote(dst, dst, ss, rs, sibling).wait_recv()

    loads = []
    for c, source in enumerate((tokens, cotangent)):
        loads.append((
            pltpu.make_async_copy(source.at[:, rows_of(z, KS)], acts_s, load_sem.at[0]),
            pltpu.make_async_copy(source.at[:, NZ * KS :], acts_d, load_sem.at[5]),
        ))

        @pl.when(core == c)
        def _(c=c):
            loads[c][0].start()
            loads[c][1].start()

    own_g = pltpu.make_async_copy(w_gate.at[0], wgu.at[:, rows_of(core, H)], load_sem.at[1])
    own_u = pltpu.make_async_copy(w_up.at[0], wgu.at[:, rows_of(core + 2, H)], load_sem.at[2])
    own_d = pltpu.make_async_copy(w_down.at[0], wd.at[rows_of(core, H), :], load_sem.at[3])
    own_c = pltpu.make_async_copy(cotangent.at[:, rows_of(z, RS)], cot_part, load_sem.at[4])
    for c in (own_g, own_u, own_d, own_c):
        c.start()

    barrier = pltpu.get_barrier_semaphore()

    def greet(device):
        pl.semaphore_signal(barrier, inc=1, device_id=device, device_id_type=MESH)

    for i in range(E):
        for dy in range(2):
            if i or dy:
                greet(dev(lax.rem(e + i, E), lax.rem(yh + dy, 2), z, core))
    for dz in range(NZ):
        for dc in range(2):
            if dz or dc:
                greet(dev(e, yh, lax.rem(z + dz, NZ), lax.rem(core + dc, 2)))

    a0 = assign_t[0:1, :]
    a1 = assign_t[1:2, :]
    w0_row = weight_t[0:1, :]
    w1_row = weight_t[1:2, :]
    expert = lax.broadcasted_iota(jnp.int32, (8, TOK), 0)
    hot0 = (expert == a0).astype(F32)
    hot1 = (expert == a1).astype(F32)
    lane = lax.broadcasted_iota(jnp.int32, (TOK, TOK), 1)
    row = lax.broadcasted_iota(jnp.int32, (TOK, TOK), 0)
    before = (row < lane).astype(BF16)
    count = jnp.dot((hot0 + hot1).astype(BF16), before, preferred_element_type=F32)
    slot0 = a0 * CAP + jnp.sum(hot0 * count, axis=0, keepdims=True).astype(jnp.int32)
    slot1 = a1 * CAP + jnp.sum(hot1 * count, axis=0, keepdims=True).astype(jnp.int32)
    slot = lax.broadcasted_iota(jnp.int32, (SLOTS, TOK), 0)
    spread0 = (slot == slot0).astype(F32)
    spread1 = (slot == slot1).astype(F32)
    spread = (spread0 + spread1).astype(BF16)
    slot_weight = jnp.sum(spread0 * w0_row + spread1 * w1_row, axis=1, keepdims=True)
    is_x = core == 0
    scale_in = jnp.where(is_x, 1.0, slot_weight)

    def dispatch(cols):
        return (scale_in * jnp.dot(spread, cols, preferred_element_type=F32)).astype(BF16)

    for c in range(2):

        @pl.when(core == c)
        def _(c=c):
            loads[c][0].wait()

    own_rows = rows_of(e, CAP)
    send_s[...] = dispatch(acts_s[...])
    xd[t, z, own_rows, :] = send_s[own_rows, :]

    pl.semaphore_wait(barrier, 2 * E - 1 + 2 * NZ - 1)

    for i in range(1, E):
        j = lax.rem(e + i, E)
        send(
            send_s.at[rows_of(j, CAP), :], xd.at[t, z, own_rows, :],
            a_send.at[i - 1], a_recv.at[i - 1], dev(j, yh, z, core),
        )

    @pl.when(core == 0)
    def _():
        remote(w_gate.at[0], wgu.at[:, 0:H], wpre_sem.at[0], wpre_sem.at[2], sibling).start()
        remote(w_up.at[0], wgu.at[:, 2 * H : 3 * H], wpre_sem.at[1], wpre_sem.at[3], sibling).start()

    @pl.when(core == 1)
    def _():
        remote(w_down.at[0], wd.at[H : 2 * H, :], wpre_sem.at[0], wpre_sem.at[2], sibling).start()

    for c in range(2):

        @pl.when(core == c)
        def _(c=c):
            loads[c][1].wait()

    for k in range(ND):
        send_d[k] = dispatch(acts_d[:, k * KS : (k + 1) * KS])
    for k in range(ND):
        xd[t, NZ + k, own_rows, :] = send_d[k, own_rows, :]
    acc_gu[...] = jnp.zeros_like(acc_gu)
    acc_h[...] = jnp.zeros_like(acc_h)
    pick0 = spread0.T.astype(BF16)
    pick1 = spread1.T.astype(BF16)
    w0 = jnp.broadcast_to(w0_row, (TOK, TOK)).T[:, 0:1]
    w1 = jnp.broadcast_to(w1_row, (TOK, TOK)).T[:, 0:1]
    on0 = jnp.where(is_x, w0, 1.0)
    on1 = jnp.where(is_x, w1, 1.0)
    for c in (own_g, own_u, own_d, own_c):
        c.wait()

    def gather(view, parts, sems):
        s_send, s_recv, b_send, b_recv = sems

        for s in range(5):
            for p in range(parts):
                for way, nxt, sign in ((0, up, -1), (1, down, 1)):
                    split = (p < parts // 2) == (way == 0)
                    if s == 4 and not split:
                        continue
                    ref = view(t, zmod(z + sign * s), p)
                    if s > 0:
                        arrived(ref, s_send.at[way, s - 1, p], s_recv.at[way, s - 1, p])
                    if s < 3 or (s == 3 and split):
                        send(ref, ref, s_send.at[way, s, p], s_recv.at[way, s, p], nxt)
                    if s > 0 or way == 0:
                        d = (sign * s) % NZ
                        send(ref, ref, b_send.at[d, p], b_recv.at[d, p], sibling)
            yield

    def sib_arrived(view, parts, sems, d):
        for p in range(parts):
            arrived(view(other, zmod(z + d), p), sems[2].at[d % NZ, p], sems[3].at[d % NZ, p])

    def xd_view(kind, zz, p):
        return xd.at[kind, zz, p * (SLOTS // NP) : (p + 1) * (SLOTS // NP), :]

    mine_g = rows_of(core, H)
    mine_u = rows_of(core + 2, H)

    def add_x(k):
        kr = rows_of(k, KS)
        acc_gu[:, 0:H] += jnp.dot(xd[0, k], wgu[kr, mine_g], preferred_element_type=F32)
        acc_gu[:, H : 2 * H] += jnp.dot(xd[0, k], wgu[kr, mine_u], preferred_element_type=F32)

    def add_y(k):
        acc_h[...] += lax.dot_general(xd[1, k], wd[mine_g, rows_of(k, KS)], NT, preferred_element_type=F32)

    def products(kind, count, index):
        @pl.when(kind == 0)
        def _():
            @pl.loop(0, count)
            def _(i):
                add_x(index(i))

        @pl.when(kind == 1)
        def _():
            @pl.loop(0, count)
            def _(i):
                add_y(index(i))

    def pair(s):
        return lambda i: zmod(z - s + 2 * s * i)

    ring_sems = (ring_send, ring_recv, sib_send, sib_recv)
    for i in range(1, E):
        src = rows_of(lax.rem(e + E - i, E), CAP)
        arrived(xd.at[t, z, src, :], a_send.at[i - 1], a_recv.at[i - 1])
    ring = gather(xd_view, NP, ring_sems)
    next(ring)
    for i in range(1, E):
        j = lax.rem(e + i, E)
        send(
            send_d.at[:, rows_of(j, CAP), :], xd.at[t, NZ:NK, own_rows, :],
            d_send.at[i - 1], d_recv.at[i - 1], dev(j, yh, z, core),
        )
    products(t, 1, lambda i: z)
    next(ring)
    products(t, 2, pair(1))
    sib_arrived(xd_view, NP, ring_sems, 0)
    products(other, 1, lambda i: z)
    next(ring)
    products(t, 2, pair(2))
    for d in (-1, 1):
        sib_arrived(xd_view, NP, ring_sems, d)
    products(other, 2, pair(1))
    next(ring)
    products(t, 2, pair(3))
    for d in (-2, 2):
        sib_arrived(xd_view, NP, ring_sems, d)
    products(other, 2, pair(2))
    for i in range(1, E):
        src = rows_of(lax.rem(e + E - i, E), CAP)
        arrived(xd.at[t, NZ:NK, src, :], d_send.at[i - 1], d_recv.at[i - 1])
    send(xd.at[t, NZ:NK], xd.at[t, NZ:NK], dsib_sem.at[0], dsib_sem.at[1], sibling)
    products(t, ND, lambda i: NZ + i)
    for d in (-3, 3):
        sib_arrived(xd_view, NP, ring_sems, d)
    products(other, 2, pair(3))
    next(ring)
    arrived(xd.at[other, NZ:NK], dsib_sem.at[0], dsib_sem.at[1])
    products(other, ND, lambda i: NZ + i)
    products(t, 1, lambda i: zmod(z + 4))
    sib_arrived(xd_view, NP, ring_sems, 4)
    products(other, 1, lambda i: zmod(z + 4))

    @pl.loop(0, E)
    def _(b):
        r = rows_of(b, CAP)
        pre_gate = acc_gu[r, 0:H]
        pre_up = acc_gu[r, H : 2 * H]
        grad_hidden = acc_h[r, :]
        sigma = jax.nn.sigmoid(pre_gate)
        silu = pre_gate * sigma
        hid[r, mine_g] = (silu * pre_up).astype(BF16)
        gpre[r, mine_g] = (grad_hidden * pre_up * sigma * (1.0 + pre_gate * (1.0 - sigma))).astype(BF16)
        gpre[r, mine_u] = (grad_hidden * silu).astype(BF16)

    @pl.when(core == 0)
    def _():
        cg = remote(gpre.at[:, 0:H], gpre.at[:, 0:H], act_sem.at[0], act_sem.at[2], sibling)
        cu = remote(gpre.at[:, 2 * H : 3 * H], gpre.at[:, 2 * H : 3 * H], act_sem.at[1], act_sem.at[3], sibling)
        cg.start()
        cu.start()
        arrived(wd.at[H : 2 * H, :], wpre_sem.at[0], wpre_sem.at[2])
        arrived(hid.at[:, H : 2 * H], act_sem.at[0], act_sem.at[2])

    @pl.when(core == 1)
    def _():
        ch = remote(hid.at[:, H : 2 * H], hid.at[:, H : 2 * H], act_sem.at[0], act_sem.at[2], sibling)
        ch.start()
        arrived(wgu.at[:, 0:H], wpre_sem.at[0], wpre_sem.at[2])
        arrived(wgu.at[:, 2 * H : 3 * H], wpre_sem.at[1], wpre_sem.at[3])
        arrived(gpre.at[:, 0:H], act_sem.at[0], act_sem.at[2])
        arrived(gpre.at[:, 2 * H : 3 * H], act_sem.at[1], act_sem.at[3])

    def term(zd):
        cols = rows_of(zd, RS)

        def keep(v):
            for q in range(NQ):
                part[q, zd] = v[:, q * QC : (q + 1) * QC].astype(BF16)

        @pl.when(core == 0)
        def _():
            keep(jnp.dot(hid[...], wd[:, cols], preferred_element_type=F32))

        @pl.when(core == 1)
        def _():
            keep(lax.dot_general(gpre[...], wgu[cols, :], NT, preferred_element_type=F32))

    def weight_grads(first, last):
        @pl.loop(first, last)
        def _(k):
            kr = rows_of(k, KS)
            g = lax.dot_general(xd[0, k], gpre[:, mine_g], TN, preferred_element_type=F32)
            gg[kr, :] = g.astype(BF16)
            u = lax.dot_general(xd[0, k], gpre[:, mine_u], TN, preferred_element_type=F32)
            gu[kr, :] = u.astype(BF16)
            w = lax.dot_general(hid[:, mine_g], xd[1, k], TN, preferred_element_type=F32)
            gd[:, kr] = w.astype(BF16)

    land = (rp, rm)

    def half(h):
        return slice(h * HALF, (h + 1) * HALF)

    def target(way, s):
        return zmod(z + 4 - s) if way == 0 else zmod(z - 4 + s)

    probs = []

    def back(q):
        def rs_start(way, s, h):
            send(
                part.at[q, target(way, s), half(h), :], land[way].at[q, s, half(h), :],
                rs_send.at[q, way * 4 + s, h], rs_recv.at[q, way * 4 + s, h], up if way == 0 else down,
            )

        def rs_arrived(way, s, h):
            arrived(land[way].at[q, s, half(h), :], rs_send.at[q, way * 4 + s, h], rs_recv.at[q, way * 4 + s, h])

        def rs_add(way, s, h):
            zd = target(way, s + 1)
            part[q, zd, half(h), :] = (
                part[q, zd, half(h), :].astype(F32) + land[way][q, s, half(h), :].astype(F32)
            ).astype(BF16)

        if q == 0:
            term(zmod(z + 4))
        rs_start(0, 0, 0)
        rs_start(1, 0, 1)
        if q == 0:
            term(zmod(z + 3))
        rs_start(0, 1, 1)
        if q == 0:
            term(zmod(z + 5))
        rs_start(1, 1, 0)
        yield
        for way, h in ((0, 0), (1, 1)):
            rs_arrived(way, 0, h)
            rs_add(way, 0, h)
            rs_start(way, 1, h)
        yield
        for s in (1, 2):
            for way, h in ((0, 1), (1, 0), (0, 0), (1, 1)):
                rs_arrived(way, s, h)
                rs_add(way, s, h)
                rs_start(way, s + 1, h)
            yield
        for h in range(2):
            for way in range(2):
                rs_arrived(way, 3, h)
            part[q, z, half(h), :] = (
                part[q, z, half(h), :].astype(F32)
                + rp[q, 3, half(h), :].astype(F32)
                + rm[q, 3, half(h), :].astype(F32)
            ).astype(BF16)
        rc[q, yh, own_rows, :] = part[q, z, own_rows, :]
        for i in range(E):
            for dy in range(2):
                if i or dy:
                    b = lax.rem(e + i, E)
                    send(
                        part.at[q, z, rows_of(b, CAP), :], rc.at[q, yh, own_rows, :],
                        c_send.at[q, i * 2 + dy], c_recv.at[q, i * 2 + dy], dev(b, lax.rem(yh + dy, 2), z, core),
                    )
        yield
        for i in range(E):
            for dy in range(2):
                if i or dy:
                    src = rows_of(lax.rem(e + E - i, E), CAP)
                    arrived(
                        rc.at[q, lax.rem(yh + dy, 2), src, :], c_send.at[q, i * 2 + dy], c_recv.at[q, i * 2 + dy]
                    )
        summed = (rc[q, 0].astype(F32) + rc[q, 1].astype(F32)).astype(BF16)
        out0 = jnp.dot(pick0, summed, preferred_element_type=F32)
        out1 = jnp.dot(pick1, summed, preferred_element_type=F32)
        outs[t, :, pl.ds(pl.multiple_of(z * RS + q * QC, QC), QC)] = (on0 * out0 + on1 * out1).astype(BF16)

        def out_view(kind, zz, p):
            return outs.at[
                kind, p * (TOK // 2) : (p + 1) * (TOK // 2), pl.ds(pl.multiple_of(zz * RS + q * QC, QC), QC)
            ]

        sems = (o_send.at[q], o_recv.at[q], osib_send.at[q], osib_recv.at[q])
        steps = gather(out_view, 2, sems)
        next(steps)
        cot = cot_part[:, q * QC : (q + 1) * QC].astype(F32)
        probs.append((jnp.sum(cot * out0, axis=1, keepdims=True), jnp.sum(cot * out1, axis=1, keepdims=True)))
        if q == NQ - 1:
            p0 = sum(v[0] for v in probs)
            p1 = sum(v[1] for v in probs)
            both = jnp.where(lane == 0, p0, 0.0) + jnp.where(lane == 1, p1, 0.0)

            @pl.when(core == 0)
            def _():
                gp[z] = both.T[0:8, :]
                for dz in range(NZ):
                    for dc in range(2):
                        if dz or dc:
                            remote(
                                gp.at[z], gp.at[z], g_send.at[dz, dc], g_recv.at[dz, dc],
                                dev(e, yh, lax.rem(z + dz, NZ), dc),
                            ).start()

        yield
        for _ in steps:
            yield
        for d in range(NZ):
            sib_arrived(out_view, 2, sems, d)
        yield

    q0, q1, q2 = (back(q) for q in range(NQ))
    next(q0)
    next(q1)

    @pl.loop(0, 5)
    def _(i):
        term(zmod(z + 6 + i))

    next(q0)
    next(q2)
    weight_grads(0, 4)
    next(q0)
    next(q1)
    weight_grads(4, 8)
    next(q0)
    next(q1)
    next(q2)
    weight_grads(8, 12)
    next(q0)
    next(q1)
    next(q2)
    for turn in ((q2, q1, q0), (q2, q0, q1), (q0, q1, q2), (q0, q1, q2), (q0, q1, q2), (q0, q1, q2), (q1, q2), (q2,)):
        for q in turn:
            next(q)

    @pl.when(core == 0)
    def _():
        for dz in range(1, NZ):
            src = zmod(z - dz)
            remote(gp.at[src], gp.at[src], g_send.at[dz, 0], g_recv.at[dz, 0], sibling).wait_recv()
        for dz in range(NZ):
            for dc in range(2):
                if dz or dc:
                    remote(gp.at[z], gp.at[z], g_send.at[dz, dc], g_recv.at[dz, dc], sibling).wait_send()

    @pl.when(core == 1)
    def _():
        for dz in range(NZ):
            src = zmod(z - dz)
            remote(gp.at[src], gp.at[src], g_send.at[dz, 1], g_recv.at[dz, 1], sibling).wait_recv()

    total = gp[0]
    for zz in range(1, NZ):
        total = total + gp[zz]
    prob[...] = total[0:2, :]

    for c in pending:
        c.wait_send()

    @pl.when(core == 0)
    def _():
        remote(w_gate.at[0], wgu.at[:, 0:H], wpre_sem.at[0], wpre_sem.at[2], sibling).wait_send()
        remote(w_up.at[0], wgu.at[:, 2 * H : 3 * H], wpre_sem.at[1], wpre_sem.at[3], sibling).wait_send()
        remote(gpre.at[:, 0:H], gpre.at[:, 0:H], act_sem.at[0], act_sem.at[2], sibling).wait_send()
        remote(gpre.at[:, 2 * H : 3 * H], gpre.at[:, 2 * H : 3 * H], act_sem.at[1], act_sem.at[3], sibling).wait_send()

    @pl.when(core == 1)
    def _():
        remote(w_down.at[0], wd.at[H : 2 * H, :], wpre_sem.at[0], wpre_sem.at[2], sibling).wait_send()
        remote(hid.at[:, H : 2 * H], hid.at[:, H : 2 * H], act_sem.at[0], act_sem.at[2], sibling).wait_send()


def store(outs, prob, gg, gu, gd, moe_out, grad_tokens, grad_prob, grad_gate, grad_up, grad_down, sem):
    copies = []
    for i, (src, dst) in enumerate((
        (gg, grad_gate.at[0]), (gu, grad_up.at[0]), (gd, grad_down.at[0]),
        (outs.at[0], moe_out), (outs.at[1], grad_tokens), (prob, grad_prob),
    )):
        copies.append(pltpu.make_async_copy(src, dst, sem.at[i]))
    for c in copies:
        c.start()
    for c in copies:
        c.wait()


def per_device(tokens, assignment, route_weight, cotangent, w_gate, w_up, w_down):
    hbm = pl.BlockSpec(memory_space=pl.ANY)
    vmem = pl.BlockSpec(memory_space=pltpu.VMEM)
    dma = pltpu.SemaphoreType.DMA
    held = pl.pallas_call(
        kernel,
        out_shape=(
            pltpu.VMEM((2, TOK, D), BF16),
            pltpu.VMEM((2, TOK), F32),
            pltpu.VMEM((D, H), BF16),
            pltpu.VMEM((D, H), BF16),
            pltpu.VMEM((H, D), BF16),
        ),
        in_specs=[hbm, vmem, vmem, hbm, hbm, hbm, hbm],
        out_specs=(vmem,) * 5,
        scratch_shapes=[
            pltpu.VMEM((TOK, KS), BF16),
            pltpu.VMEM((TOK, ND * KS), BF16),
            pltpu.VMEM((TOK, RS), BF16),
            pltpu.VMEM((D, 4 * H), BF16),
            pltpu.VMEM((2 * H, D), BF16),
            pltpu.VMEM((SLOTS, KS), BF16),
            pltpu.VMEM((ND, SLOTS, KS), BF16),
            pltpu.VMEM((2, NK, SLOTS, KS), BF16),
            pltpu.VMEM((SLOTS, 2 * H), F32),
            pltpu.VMEM((SLOTS, H), F32),
            pltpu.VMEM((SLOTS, 2 * H), BF16),
            pltpu.VMEM((SLOTS, 4 * H), BF16),
            pltpu.VMEM((NQ, NZ, SLOTS, QC), BF16),
            pltpu.VMEM((NQ, 4, SLOTS, QC), BF16),
            pltpu.VMEM((NQ, 4, SLOTS, QC), BF16),
            pltpu.VMEM((NQ, 2, SLOTS, QC), BF16),
            pltpu.VMEM((NZ, 8, TOK), F32),
            dma((6,)), dma((4,)),
            dma((E - 1,)), dma((E - 1,)), dma((E - 1,)), dma((E - 1,)),
            dma((2, 4, NP)), dma((2, 4, NP)), dma((NZ, NP)), dma((NZ, NP)), dma((2,)),
            dma((4,)), dma((NQ, 8, 2)), dma((NQ, 8, 2)), dma((NQ, 2 * E)), dma((NQ, 2 * E)),
            dma((NQ, 2, 4, 2)), dma((NQ, 2, 4, 2)), dma((NQ, NZ, 2)), dma((NQ, NZ, 2)),
            dma((NZ, 2)), dma((NZ, 2)),
        ],
        compiler_params=pltpu.CompilerParams(
            collective_id=0, has_side_effects=True, vmem_limit_bytes=50 * 1024 * 1024
        ),
    )(tokens, assignment.T, route_weight.T, cotangent, w_gate, w_up, w_down)
    moe_out, grad_tokens, grad_prob, grad_gate, grad_up, grad_down = pl.pallas_call(
        store,
        out_shape=(
            jax.ShapeDtypeStruct((TOK, D), BF16),
            jax.ShapeDtypeStruct((TOK, D), BF16),
            jax.ShapeDtypeStruct((2, TOK), F32),
            jax.ShapeDtypeStruct((1, D, H), BF16),
            jax.ShapeDtypeStruct((1, D, H), BF16),
            jax.ShapeDtypeStruct((1, H, D), BF16),
        ),
        in_specs=[vmem] * 5,
        out_specs=(hbm,) * 6,
        scratch_shapes=[dma((6,))],
        compiler_params=pltpu.CompilerParams(vmem_limit_bytes=16 * 1024 * 1024),
    )(*held)
    return (moe_out, grad_tokens, grad_prob.T, grad_gate, grad_up, grad_down)


def solution(mesh):
    return jax.shard_map(
        per_device,
        mesh=mesh,
        in_specs=(
            P("expert", None),
            P("expert", None),
            P("expert", None),
            P("expert", None),
            P("expert", None, "fsdp"),
            P("expert", None, "fsdp"),
            P("expert", "fsdp", None),
        ),
        out_specs=(
            P("expert", None),
            P("expert", None),
            P("expert", None),
            P("expert", None, "fsdp"),
            P("expert", None, "fsdp"),
            P("expert", "fsdp", None),
        ),
        check_vma=False,
    )
```

```python
import jax
import jax.numpy as jnp
from jax import lax
from jax.experimental import pallas as pl
from jax.experimental.pallas import tpu as pltpu
from jax.sharding import PartitionSpec as P

MESH = pl.DeviceIdType.MESH
BF16 = jnp.bfloat16
F32 = jnp.float32
NT = (((1,), (1,)), ((), ()))
TN = (((0,), (0,)), ((), ()))

E = 8
NZ = 8
CAP = 48
TOK = 128
SLOTS = E * CAP
D = 3072
H = 256
HALF = SLOTS // 2
KS = 256
NK = D // KS
ND = NK - NZ
RS = D // NZ
QC = 128
NQ = RS // QC
NP = 4


def rows_of(index, size):
    return pl.ds(pl.multiple_of(index * size, size), size)


def kernel(
    tokens, assign_t, weight_t, cotangent, w_gate, w_up, w_down,
    outs, prob, gg, gu, gd,
    acts_s, acts_d, cot_part, wgu, wd, send_s, send_d, xd, acc_gu, acc_h, hid, gpre,
    part, rp, rm, rc, gp, gp_sum,
    load_sem, wpre_sem,
    a_send, a_recv, d_send, d_recv, ring_send, ring_recv, sib_send, sib_recv, dsib_sem,
    act_sem, rs_send, rs_recv, c_send, c_recv, o_send, o_recv, osib_send, osib_recv, g_send, g_recv, gsum_sem,
):
    e = lax.axis_index("expert")
    f = lax.axis_index("fsdp")
    core = lax.rem(f, 2)
    z = lax.rem(lax.div(f, 2), NZ)
    yh = lax.div(f, 2 * NZ)

    def dev(e_, yh_, z_, c_):
        return (e_, yh_ * (2 * NZ) + z_ * 2 + c_)

    sibling = dev(e, yh, z, 1 - core)
    up = dev(e, yh, lax.rem(z + 1, NZ), core)
    down = dev(e, yh, lax.rem(z + NZ - 1, NZ), core)

    def zmod(v):
        return lax.rem(v + 2 * NZ, NZ)

    def remote(src, dst, ss, rs, device):
        return pltpu.make_async_remote_copy(
            src_ref=src, dst_ref=dst, send_sem=ss, recv_sem=rs, device_id=device, device_id_type=MESH
        )

    def arrived(dst, ss, rs):
        remote(dst, dst, ss, rs, sibling).wait_recv()

    loads = []
    for c, source in enumerate((tokens, cotangent)):
        loads.append((
            pltpu.make_async_copy(source.at[:, rows_of(z, KS)], acts_s, load_sem.at[0]),
            pltpu.make_async_copy(source.at[:, NZ * KS :], acts_d, load_sem.at[5]),
        ))

        @pl.when(core == c)
        def _(c=c):
            loads[c][0].start()
            loads[c][1].start()

    own_g = pltpu.make_async_copy(w_gate.at[0], wgu.at[:, rows_of(core, H)], load_sem.at[1])
    own_u = pltpu.make_async_copy(w_up.at[0], wgu.at[:, rows_of(core + 2, H)], load_sem.at[2])
    own_d = pltpu.make_async_copy(w_down.at[0], wd.at[rows_of(core, H), :], load_sem.at[3])
    own_c = pltpu.make_async_copy(cotangent.at[:, rows_of(z, RS)], cot_part, load_sem.at[4])
    for c in (own_g, own_u, own_d, own_c):
        c.start()

    barrier = pltpu.get_barrier_semaphore()

    def greet(device):
        pl.semaphore_signal(barrier, inc=1, device_id=device, device_id_type=MESH)

    greet(sibling)
    for i in range(E):
        for dy in range(2):
            if i or dy:
                greet(dev(lax.rem(e + i, E), lax.rem(yh + dy, 2), z, core))
    for dz in range(1, NZ):
        greet(dev(e, yh, lax.rem(z + dz, NZ), core))

    a0 = assign_t[0:1, :]
    a1 = assign_t[1:2, :]
    w0_row = weight_t[0:1, :]
    w1_row = weight_t[1:2, :]
    expert = lax.broadcasted_iota(jnp.int32, (8, TOK), 0)
    hot0 = (expert == a0).astype(F32)
    hot1 = (expert == a1).astype(F32)
    lane = lax.broadcasted_iota(jnp.int32, (TOK, TOK), 1)
    row = lax.broadcasted_iota(jnp.int32, (TOK, TOK), 0)
    before = (row < lane).astype(BF16)
    count = jnp.dot((hot0 + hot1).astype(BF16), before, preferred_element_type=F32)
    slot0 = a0 * CAP + jnp.sum(hot0 * count, axis=0, keepdims=True).astype(jnp.int32)
    slot1 = a1 * CAP + jnp.sum(hot1 * count, axis=0, keepdims=True).astype(jnp.int32)
    slot = lax.broadcasted_iota(jnp.int32, (SLOTS, TOK), 0)
    spread0 = (slot == slot0).astype(F32)
    spread1 = (slot == slot1).astype(F32)
    spread = (spread0 + spread1).astype(BF16)
    own_rows = rows_of(e, CAP)
    mine_g = rows_of(core, H)
    mine_u = rows_of(core + 2, H)
    land = (rp, rm)

    def half(h):
        return slice(h * HALF, (h + 1) * HALF)

    def target(way, s):
        return zmod(z + 4 - s) if way == 0 else zmod(z - 4 + s)

    def xd_view(kind, zz, p):
        return xd.at[kind, zz, p * (SLOTS // NP) : (p + 1) * (SLOTS // NP), :]

    ring_sems = (ring_send, ring_recv, sib_send, sib_recv)

    def sib_arrived(view, kind, parts, sems, d):
        for p in range(parts):
            arrived(view(kind, zmod(z + d), p), sems[2].at[d % NZ, p], sems[3].at[d % NZ, p])

    def add_x(k):
        kr = rows_of(k, KS)
        acc_gu[:, 0:H] += jnp.dot(xd[0, k], wgu[kr, mine_g], preferred_element_type=F32)
        acc_gu[:, H : 2 * H] += jnp.dot(xd[0, k], wgu[kr, mine_u], preferred_element_type=F32)

    def add_y(k):
        acc_h[...] += lax.dot_general(xd[1, k], wd[mine_g, rows_of(k, KS)], NT, preferred_element_type=F32)

    def add_pair(add, s):
        @pl.loop(0, 2)
        def _(i):
            add(zmod(z - s + 2 * s * i))

    def add_direct(add):
        @pl.loop(NZ, NK)
        def _(k):
            add(k)

    def forward():
        @pl.loop(0, E)
        def _(b):
            r = rows_of(b, CAP)
            pre_gate = acc_gu[r, 0:H]
            hid[r, mine_g] = (pre_gate * jax.nn.sigmoid(pre_gate) * acc_gu[r, H : 2 * H]).astype(BF16)

    def backward():
        @pl.loop(0, E)
        def _(b):
            r = rows_of(b, CAP)
            pre_gate = acc_gu[r, 0:H]
            grad_hidden = acc_h[r, :]
            sigma = jax.nn.sigmoid(pre_gate)
            gpre[r, mine_g] = (
                grad_hidden * acc_gu[r, H : 2 * H] * sigma * (1.0 + pre_gate * (1.0 - sigma))
            ).astype(BF16)
            gpre[r, mine_u] = (grad_hidden * (pre_gate * sigma)).astype(BF16)

    def weight_grads(first, last):
        @pl.loop(first, last)
        def _(k):
            kr = rows_of(k, KS)
            g = lax.dot_general(xd[0, k], gpre[:, mine_g], TN, preferred_element_type=F32)
            gg[kr, :] = g.astype(BF16)
            u = lax.dot_general(xd[0, k], gpre[:, mine_u], TN, preferred_element_type=F32)
            gu[kr, :] = u.astype(BF16)
            w = lax.dot_general(hid[:, mine_g], xd[1, k], TN, preferred_element_type=F32)
            gd[:, kr] = w.astype(BF16)

    def program(t):
        pending = []

        def send(src, dst, ss, rs, device):
            c = remote(src, dst, ss, rs, device)
            c.start()
            pending.append(c)

        if t == 1:
            slot_weight = jnp.sum(spread0 * w0_row + spread1 * w1_row, axis=1, keepdims=True)

        def dispatch(cols):
            v = jnp.dot(spread, cols, preferred_element_type=F32)
            return (v if t == 0 else slot_weight * v).astype(BF16)

        def exchange_slice():
            for i in range(1, E):
                j = lax.rem(e + i, E)
                send(
                    send_s.at[rows_of(j, CAP), :], xd.at[t, z, own_rows, :],
                    a_send.at[i - 1], a_recv.at[i - 1], dev(j, yh, z, core),
                )

        def slice_arrived():
            for i in range(1, E):
                src = rows_of(lax.rem(e + E - i, E), CAP)
                arrived(xd.at[t, z, src, :], a_send.at[i - 1], a_recv.at[i - 1])

        def exchange_direct():
            for i in range(1, E):
                j = lax.rem(e + i, E)
                send(
                    send_d.at[:, rows_of(j, CAP), :], xd.at[t, NZ:NK, own_rows, :],
                    d_send.at[i - 1], d_recv.at[i - 1], dev(j, yh, z, core),
                )

        def direct_arrived():
            for i in range(1, E):
                src = rows_of(lax.rem(e + E - i, E), CAP)
                arrived(xd.at[t, NZ:NK, src, :], d_send.at[i - 1], d_recv.at[i - 1])
            send(xd.at[t, NZ:NK], xd.at[t, NZ:NK], dsib_sem.at[0], dsib_sem.at[1], sibling)

        def gather(view, parts, sems):
            s_send, s_recv, b_send, b_recv = sems

            for s in range(5):
                for p in range(parts):
                    for way, nxt, sign in ((0, up, -1), (1, down, 1)):
                        split = (p < parts // 2) == (way == 0)
                        if s == 4 and not split:
                            continue
                        ref = view(t, zmod(z + sign * s), p)
                        if s > 0:
                            arrived(ref, s_send.at[way, s - 1, p], s_recv.at[way, s - 1, p])
                        if s < 3 or (s == 3 and split):
                            send(ref, ref, s_send.at[way, s, p], s_recv.at[way, s, p], nxt)
                        if s > 0 or way == 0:
                            d = (sign * s) % NZ
                            send(ref, ref, b_send.at[d, p], b_recv.at[d, p], sibling)
                yield

        def scatter(view, sems):
            s_send, s_recv, b_send, b_recv = sems
            ref = view(t, z)
            for dz in (4, 3, 5, 2, 6, 1, 7):
                to = dev(e, yh, lax.rem(z + dz, NZ), core)
                send(ref, ref, s_send.at[dz // 4, dz % 4, 0], s_recv.at[dz // 4, dz % 4, 0], to)
            send(ref, ref, b_send.at[0, 0], b_recv.at[0, 0], sibling)
            yield
            for dz in (1, 7, 2, 6, 3, 5, 4):
                ref = view(t, zmod(z - dz))
                arrived(ref, s_send.at[dz // 4, dz % 4, 0], s_recv.at[dz // 4, dz % 4, 0])
                send(ref, ref, b_send.at[NZ - dz, 0], b_recv.at[NZ - dz, 0], sibling)
            yield

        def term(zd):
            cols = rows_of(zd, RS)
            if t == 0:
                v = jnp.dot(hid[...], wd[:, cols], preferred_element_type=F32)
            else:
                v = lax.dot_general(gpre[...], wgu[cols, :], NT, preferred_element_type=F32)
            for q in range(NQ):
                part[q, zd] = v[:, q * QC : (q + 1) * QC].astype(BF16)

        def other_terms():
            @pl.loop(0, 5)
            def _(i):
                term(zmod(z + 6 + i))

        probs = []

        def back(q):
            def rs_start(way, s, h):
                send(
                    part.at[q, target(way, s), half(h), :], land[way].at[q, s, half(h), :],
                    rs_send.at[q, way * 4 + s, h], rs_recv.at[q, way * 4 + s, h], up if way == 0 else down,
                )

            def rs_arrived(way, s, h):
                arrived(land[way].at[q, s, half(h), :], rs_send.at[q, way * 4 + s, h], rs_recv.at[q, way * 4 + s, h])

            def rs_add(way, s, h):
                zd = target(way, s + 1)
                part[q, zd, half(h), :] = (
                    part[q, zd, half(h), :].astype(F32) + land[way][q, s, half(h), :].astype(F32)
                ).astype(BF16)

            if q == 0:
                term(zmod(z + 4))
            rs_start(0, 0, 0)
            rs_start(1, 0, 1)
            if q == 0:
                term(zmod(z + 3))
            rs_start(0, 1, 1)
            if q == 0:
                term(zmod(z + 5))
            rs_start(1, 1, 0)
            yield
            for way, h in ((0, 0), (1, 1)):
                rs_arrived(way, 0, h)
                rs_add(way, 0, h)
                rs_start(way, 1, h)
            yield
            for s in (1, 2):
                for way, h in ((0, 1), (1, 0), (0, 0), (1, 1)):
                    rs_arrived(way, s, h)
                    rs_add(way, s, h)
                    rs_start(way, s + 1, h)
                yield
            for h in range(2):
                for way in range(2):
                    rs_arrived(way, 3, h)
                part[q, z, half(h), :] = (
                    part[q, z, half(h), :].astype(F32)
                    + rp[q, 3, half(h), :].astype(F32)
                    + rm[q, 3, half(h), :].astype(F32)
                ).astype(BF16)
            rc[q, yh, own_rows, :] = part[q, z, own_rows, :]
            for i in range(E):
                for dy in range(2):
                    if i or dy:
                        b = lax.rem(e + i, E)
                        send(
                            part.at[q, z, rows_of(b, CAP), :], rc.at[q, yh, own_rows, :],
                            c_send.at[q, i * 2 + dy], c_recv.at[q, i * 2 + dy],
                            dev(b, lax.rem(yh + dy, 2), z, core),
                        )
            yield
            for i in range(E):
                for dy in range(2):
                    if i or dy:
                        src = rows_of(lax.rem(e + E - i, E), CAP)
                        arrived(
                            rc.at[q, lax.rem(yh + dy, 2), src, :],
                            c_send.at[q, i * 2 + dy], c_recv.at[q, i * 2 + dy],
                        )
            summed = (rc[q, 0].astype(F32) + rc[q, 1].astype(F32)).astype(BF16)
            out0 = jnp.dot(pick0, summed, preferred_element_type=F32)
            out1 = jnp.dot(pick1, summed, preferred_element_type=F32)
            mixed = w0 * out0 + w1 * out1 if t == 0 else out0 + out1
            outs[t, :, pl.ds(pl.multiple_of(z * RS + q * QC, QC), QC)] = mixed.astype(BF16)

            def columns(zz):
                return pl.ds(pl.multiple_of(zz * RS + q * QC, QC), QC)

            def half_view(kind, zz, p):
                return outs.at[kind, p * (TOK // 2) : (p + 1) * (TOK // 2), columns(zz)]

            def whole_view(kind, zz, p=0):
                return outs.at[kind, :, columns(zz)]

            sems = (o_send.at[q], o_recv.at[q], osib_send.at[q], osib_recv.at[q])
            straight = q >= NQ - 1 - t
            steps = scatter(whole_view, sems) if straight else gather(half_view, 2, sems)
            next(steps)
            if t == 0:
                cot = cot_part[:, q * QC : (q + 1) * QC].astype(F32)
                probs.append((jnp.sum(cot * out0, axis=1, keepdims=True), jnp.sum(cot * out1, axis=1, keepdims=True)))
                if q == NQ - 1:
                    p0 = sum(v[0] for v in probs)
                    p1 = sum(v[1] for v in probs)
                    gp[z] = (jnp.where(lane == 0, p0, 0.0) + jnp.where(lane == 1, p1, 0.0)).T[0:8, :]
                    for dz in range(1, NZ):
                        send(gp.at[z], gp.at[z], g_send.at[dz], g_recv.at[dz], dev(e, yh, lax.rem(z + dz, NZ), core))
            yield
            for _ in steps:
                yield
            for d in range(NZ):
                if q >= NQ - 2 + t:
                    sib_arrived(whole_view, 1 - t, 1, sems, d)
                else:
                    sib_arrived(half_view, 1 - t, 2, sems, d)
            yield

        loads[t][0].wait()
        send_s[...] = dispatch(acts_s[...])
        xd[t, z, own_rows, :] = send_s[own_rows, :]
        pl.semaphore_wait(barrier, 2 * E - 1 + NZ)
        if t == 0:
            exchange_slice()
            send(w_gate.at[0], wgu.at[:, 0:H], wpre_sem.at[0], wpre_sem.at[2], sibling)
            send(w_up.at[0], wgu.at[:, 2 * H : 3 * H], wpre_sem.at[1], wpre_sem.at[3], sibling)
        else:
            send(w_down.at[0], wd.at[H : 2 * H, :], wpre_sem.at[0], wpre_sem.at[2], sibling)
        loads[t][1].wait()
        for k in range(ND):
            send_d[k] = dispatch(acts_d[:, k * KS : (k + 1) * KS])
        for k in range(ND):
            xd[t, NZ + k, own_rows, :] = send_d[k, own_rows, :]
        acc_gu[...] = jnp.zeros_like(acc_gu)
        acc_h[...] = jnp.zeros_like(acc_h)
        pick0 = spread0.T.astype(BF16)
        pick1 = spread1.T.astype(BF16)
        if t == 0:
            w0 = jnp.broadcast_to(w0_row, (TOK, TOK)).T[:, 0:1]
            w1 = jnp.broadcast_to(w1_row, (TOK, TOK)).T[:, 0:1]
        for c in (own_g, own_u, own_d, own_c):
            c.wait()
        ring = gather(xd_view, NP, ring_sems)
        q0, q1, q2 = (back(q) for q in range(NQ))

        def go(*order):
            for q in order:
                next(q)

        def sib_slices(*ds):
            for d in ds:
                sib_arrived(xd_view, 1 - t, NP, ring_sems, d)

        if t == 0:
            slice_arrived()
            go(ring)
            exchange_direct()
            add_x(z)
            go(ring)
            add_pair(add_x, 1)
            go(ring)
            add_pair(add_x, 2)
            go(ring)
            add_pair(add_x, 3)
            direct_arrived()
            add_direct(add_x)
            go(ring)
            add_x(zmod(z + 4))
            forward()
            arrived(wd.at[H : 2 * H, :], wpre_sem.at[0], wpre_sem.at[2])
            arrived(hid.at[:, H : 2 * H], act_sem.at[0], act_sem.at[2])
            go(q0, q1)
            other_terms()
            go(q2)
            sib_slices(0, 1, -1)
            add_y(z)
            add_pair(add_y, 1)
            go(q0)
            sib_slices(2, -2)
            add_pair(add_y, 2)
            go(q1)
            sib_slices(3, -3)
            add_pair(add_y, 3)
            arrived(xd.at[1, NZ:NK], dsib_sem.at[0], dsib_sem.at[1])
            add_direct(add_y)
            go(q2)
            sib_slices(4)
            add_y(zmod(z + 4))
            backward()
            send(gpre.at[:, 0:H], gpre.at[:, 0:H], act_sem.at[0], act_sem.at[2], sibling)
            send(gpre.at[:, 2 * H : 3 * H], gpre.at[:, 2 * H : 3 * H], act_sem.at[1], act_sem.at[3], sibling)
            go(q0, q1, q2)
            weight_grads(0, 4)
            go(q0, q1, q2)
            weight_grads(4, 8)
            go(q0, q1, q2)
            weight_grads(8, 12)
            go(q0, q1, q2, q0, q1, q0, q1, q2, q0, q1, q0, q1)
            for dz in range(1, NZ):
                arrived(gp.at[zmod(z - dz)], g_send.at[dz], g_recv.at[dz])
            total = gp[0]
            for zz in range(1, NZ):
                total = total + gp[zz]
            gp_sum[...] = total
            send(gp_sum, gp_sum, gsum_sem.at[0], gsum_sem.at[1], sibling)
            go(q0, q1, q2)
        else:
            sib_slices(0)
            exchange_slice()
            add_x(z)
            sib_slices(1, -1)
            add_pair(add_x, 1)
            slice_arrived()
            sib_slices(2, -2)
            add_pair(add_x, 2)
            sib_slices(3, -3)
            go(ring)
            exchange_direct()
            add_pair(add_x, 3)
            arrived(xd.at[0, NZ:NK], dsib_sem.at[0], dsib_sem.at[1])
            add_direct(add_x)
            sib_slices(4)
            add_x(zmod(z + 4))
            forward()
            send(hid.at[:, H : 2 * H], hid.at[:, H : 2 * H], act_sem.at[0], act_sem.at[2], sibling)
            go(ring)
            add_y(z)
            add_pair(add_y, 1)
            go(ring)
            add_pair(add_y, 2)
            go(ring)
            add_pair(add_y, 3)
            direct_arrived()
            add_direct(add_y)
            go(ring)
            add_y(zmod(z + 4))
            backward()
            arrived(wgu.at[:, 0:H], wpre_sem.at[0], wpre_sem.at[2])
            arrived(wgu.at[:, 2 * H : 3 * H], wpre_sem.at[1], wpre_sem.at[3])
            arrived(gpre.at[:, 0:H], act_sem.at[0], act_sem.at[2])
            arrived(gpre.at[:, 2 * H : 3 * H], act_sem.at[1], act_sem.at[3])
            go(q0, q1)
            other_terms()
            go(q0, q2)
            weight_grads(0, 4)
            go(q0, q1)
            weight_grads(4, 8)
            go(q0, q1, q2)
            weight_grads(8, 12)
            go(q0, q1, q2, q2, q1, q0, q2, q1, q0, q0, q2, q0, q0, q1, q2, q0, q1, q2)
            arrived(gp_sum, gsum_sem.at[0], gsum_sem.at[1])

        for q in (ring, q0, q1, q2):
            assert next(q, None) is None
        prob[...] = gp_sum[0:2, :]
        for c in pending:
            c.wait_send()

    for c in range(2):

        @pl.when(core == c)
        def _(c=c):
            program(c)


def store(outs, prob, gg, gu, gd, moe_out, grad_tokens, grad_prob, grad_gate, grad_up, grad_down, sem):
    copies = []
    for i, (src, dst) in enumerate((
        (gg, grad_gate.at[0]), (gu, grad_up.at[0]), (gd, grad_down.at[0]),
        (outs.at[0], moe_out), (outs.at[1], grad_tokens), (prob, grad_prob),
    )):
        copies.append(pltpu.make_async_copy(src, dst, sem.at[i]))
    for c in copies:
        c.start()
    for c in copies:
        c.wait()


def per_device(tokens, assignment, route_weight, cotangent, w_gate, w_up, w_down):
    hbm = pl.BlockSpec(memory_space=pl.ANY)
    vmem = pl.BlockSpec(memory_space=pltpu.VMEM)
    dma = pltpu.SemaphoreType.DMA
    held = pl.pallas_call(
        kernel,
        out_shape=(
            pltpu.VMEM((2, TOK, D), BF16),
            pltpu.VMEM((2, TOK), F32),
            pltpu.VMEM((D, H), BF16),
            pltpu.VMEM((D, H), BF16),
            pltpu.VMEM((H, D), BF16),
        ),
        in_specs=[hbm, vmem, vmem, hbm, hbm, hbm, hbm],
        out_specs=(vmem,) * 5,
        scratch_shapes=[
            pltpu.VMEM((TOK, KS), BF16),
            pltpu.VMEM((TOK, ND * KS), BF16),
            pltpu.VMEM((TOK, RS), BF16),
            pltpu.VMEM((D, 4 * H), BF16),
            pltpu.VMEM((2 * H, D), BF16),
            pltpu.VMEM((SLOTS, KS), BF16),
            pltpu.VMEM((ND, SLOTS, KS), BF16),
            pltpu.VMEM((2, NK, SLOTS, KS), BF16),
            pltpu.VMEM((SLOTS, 2 * H), F32),
            pltpu.VMEM((SLOTS, H), F32),
            pltpu.VMEM((SLOTS, 2 * H), BF16),
            pltpu.VMEM((SLOTS, 4 * H), BF16),
            pltpu.VMEM((NQ, NZ, SLOTS, QC), BF16),
            pltpu.VMEM((NQ, 4, SLOTS, QC), BF16),
            pltpu.VMEM((NQ, 4, SLOTS, QC), BF16),
            pltpu.VMEM((NQ, 2, SLOTS, QC), BF16),
            pltpu.VMEM((NZ, 8, TOK), F32),
            pltpu.VMEM((8, TOK), F32),
            dma((6,)), dma((4,)),
            dma((E - 1,)), dma((E - 1,)), dma((E - 1,)), dma((E - 1,)),
            dma((2, 4, NP)), dma((2, 4, NP)), dma((NZ, NP)), dma((NZ, NP)), dma((2,)),
            dma((4,)), dma((NQ, 8, 2)), dma((NQ, 8, 2)), dma((NQ, 2 * E)), dma((NQ, 2 * E)),
            dma((NQ, 2, 4, 2)), dma((NQ, 2, 4, 2)), dma((NQ, NZ, 2)), dma((NQ, NZ, 2)),
            dma((NZ,)), dma((NZ,)), dma((2,)),
        ],
        compiler_params=pltpu.CompilerParams(
            collective_id=0, has_side_effects=True, vmem_limit_bytes=50 * 1024 * 1024
        ),
    )(tokens, assignment.T, route_weight.T, cotangent, w_gate, w_up, w_down)
    moe_out, grad_tokens, grad_prob, grad_gate, grad_up, grad_down = pl.pallas_call(
        store,
        out_shape=(
            jax.ShapeDtypeStruct((TOK, D), BF16),
            jax.ShapeDtypeStruct((TOK, D), BF16),
            jax.ShapeDtypeStruct((2, TOK), F32),
            jax.ShapeDtypeStruct((1, D, H), BF16),
            jax.ShapeDtypeStruct((1, D, H), BF16),
            jax.ShapeDtypeStruct((1, H, D), BF16),
        ),
        in_specs=[vmem] * 5,
        out_specs=(hbm,) * 6,
        scratch_shapes=[dma((6,))],
        compiler_params=pltpu.CompilerParams(vmem_limit_bytes=16 * 1024 * 1024),
    )(*held)
    return (moe_out, grad_tokens, grad_prob.T, grad_gate, grad_up, grad_down)


def solution(mesh):
    return jax.shard_map(
        per_device,
        mesh=mesh,
        in_specs=(
            P("expert", None),
            P("expert", None),
            P("expert", None),
            P("expert", None),
            P("expert", None, "fsdp"),
            P("expert", None, "fsdp"),
            P("expert", "fsdp", None),
        ),
        out_specs=(
            P("expert", None),
            P("expert", None),
            P("expert", None),
            P("expert", None, "fsdp"),
            P("expert", None, "fsdp"),
            P("expert", "fsdp", None),
        ),
        check_vma=False,
    )
```

```python
import jax
import jax.numpy as jnp
from jax import lax
from jax.experimental import pallas as pl
from jax.experimental.pallas import tpu as pltpu
from jax.sharding import PartitionSpec as P

MESH = pl.DeviceIdType.MESH
BF16 = jnp.bfloat16
F32 = jnp.float32
NT = (((1,), (1,)), ((), ()))
TN = (((0,), (0,)), ((), ()))

E = 8
NZ = 8
CAP = 48
TOK = 128
SLOTS = E * CAP
D = 3072
H = 256
HALF = SLOTS // 2
NG = 4
KG = D // NG
RS = D // NZ
QC = 128
NQ = RS // QC
NP = 4


def rows_of(index, size):
    return pl.ds(pl.multiple_of(index * size, size), size)


def kernel(
    tokens, assign_t, weight_t, cotangent, w_gate, w_up, w_down,
    outs, prob, gg, gu, gd,
    acts, cot_part, wgu, wd, send_x, send_y, xg, yd, acc_gu, acc_h, hid, gpre,
    part, rp, rm, rc, gp, gp_sum,
    load_sem, wpre_sem,
    a_send, a_recv, d_send, d_recv, ring_send, ring_recv, sib_send, sib_recv, dsib_send, dsib_recv,
    act_sem, rs_send, rs_recv, c_send, c_recv, o_send, o_recv, osib_send, osib_recv, g_send, g_recv, gsum_sem,
):
    e = lax.axis_index("expert")
    f = lax.axis_index("fsdp")
    core = lax.rem(f, 2)
    z = lax.rem(lax.div(f, 2), NZ)
    yh = lax.div(f, 2 * NZ)

    def dev(e_, yh_, z_, c_):
        return (e_, yh_ * (2 * NZ) + z_ * 2 + c_)

    sibling = dev(e, yh, z, 1 - core)
    up = dev(e, yh, lax.rem(z + 1, NZ), core)
    down = dev(e, yh, lax.rem(z + NZ - 1, NZ), core)

    def zmod(v):
        return lax.rem(v + 2 * NZ, NZ)

    def remote(src, dst, ss, rs, device):
        return pltpu.make_async_remote_copy(
            src_ref=src, dst_ref=dst, send_sem=ss, recv_sem=rs, device_id=device, device_id_type=MESH
        )

    def arrived(dst, ss, rs):
        remote(dst, dst, ss, rs, sibling).wait_recv()

    load_x = [
        pltpu.make_async_copy(tokens.at[:, g * KG : (g + 1) * KG], acts.at[g], load_sem.at[5 + g]) for g in range(NG)
    ]
    own_c = pltpu.make_async_copy(cotangent.at[:, rows_of(z, RS)], cot_part, load_sem.at[4])
    own_c.start()

    @pl.when(core == 0)
    def _():
        for c in load_x:
            c.start()

    own_g = pltpu.make_async_copy(w_gate.at[0], wgu.at[:, rows_of(core, H)], load_sem.at[1])
    own_u = pltpu.make_async_copy(w_up.at[0], wgu.at[:, rows_of(core + 2, H)], load_sem.at[2])
    own_d = pltpu.make_async_copy(w_down.at[0], wd.at[rows_of(core, H), :], load_sem.at[3])
    for c in (own_g, own_u, own_d):
        c.start()

    barrier = pltpu.get_barrier_semaphore()

    def greet(device):
        pl.semaphore_signal(barrier, inc=1, device_id=device, device_id_type=MESH)

    greet(sibling)
    for i in range(E):
        for dy in range(2):
            if i or dy:
                greet(dev(lax.rem(e + i, E), lax.rem(yh + dy, 2), z, core))
    for dz in range(1, NZ):
        greet(dev(e, yh, lax.rem(z + dz, NZ), core))

    a0 = assign_t[0:1, :]
    a1 = assign_t[1:2, :]
    w0_row = weight_t[0:1, :]
    w1_row = weight_t[1:2, :]
    expert = lax.broadcasted_iota(jnp.int32, (8, TOK), 0)
    hot0 = (expert == a0).astype(F32)
    hot1 = (expert == a1).astype(F32)
    lane = lax.broadcasted_iota(jnp.int32, (TOK, TOK), 1)
    row = lax.broadcasted_iota(jnp.int32, (TOK, TOK), 0)
    before = (row < lane).astype(BF16)
    count = jnp.dot((hot0 + hot1).astype(BF16), before, preferred_element_type=F32)
    slot0 = a0 * CAP + jnp.sum(hot0 * count, axis=0, keepdims=True).astype(jnp.int32)
    slot1 = a1 * CAP + jnp.sum(hot1 * count, axis=0, keepdims=True).astype(jnp.int32)
    slot = lax.broadcasted_iota(jnp.int32, (SLOTS, TOK), 0)
    spread0 = (slot == slot0).astype(F32)
    spread1 = (slot == slot1).astype(F32)
    spread = (spread0 + spread1).astype(BF16)
    own_rows = rows_of(e, CAP)
    mine_g = rows_of(core, H)
    mine_u = rows_of(core + 2, H)
    land = (rp, rm)

    def half(h):
        return slice(h * HALF, (h + 1) * HALF)

    def target(way, s):
        return zmod(z + 4 - s) if way == 0 else zmod(z - 4 + s)

    def yd_view(zz, p):
        return yd.at[zz, p * (SLOTS // NP) : (p + 1) * (SLOTS // NP), :]

    partners = ((1, 0), (3, 0), (0, 1), (2, 0), (1, 1), (3, 1), (2, 1))
    ey = lax.div(e, 4)
    ex = lax.rem(e, 4)

    def group_of(dx, dy):
        return lax.rem(ey + dy, 2) * 4 + lax.rem(ex + dx, 4)

    def add_x(g):
        kr = rows_of(g, KG)
        acc_gu[:, 0:H] += jnp.dot(xg[g], wgu[kr, mine_g], preferred_element_type=F32)
        acc_gu[:, H : 2 * H] += jnp.dot(xg[g], wgu[kr, mine_u], preferred_element_type=F32)

    def add_y(k):
        acc_h[...] += lax.dot_general(yd[k], wd[mine_g, rows_of(k, RS)], NT, preferred_element_type=F32)

    def add_pair(s):
        @pl.loop(0, 2)
        def _(i):
            add_y(zmod(z - s + 2 * s * i))

    def forward():
        @pl.loop(0, E)
        def _(b):
            r = rows_of(b, CAP)
            pre_gate = acc_gu[r, 0:H]
            hid[r, mine_g] = (pre_gate * jax.nn.sigmoid(pre_gate) * acc_gu[r, H : 2 * H]).astype(BF16)

    def backward():
        @pl.loop(0, E)
        def _(b):
            r = rows_of(b, CAP)
            pre_gate = acc_gu[r, 0:H]
            grad_hidden = acc_h[r, :]
            sigma = jax.nn.sigmoid(pre_gate)
            gpre[r, mine_g] = (
                grad_hidden * acc_gu[r, H : 2 * H] * sigma * (1.0 + pre_gate * (1.0 - sigma))
            ).astype(BF16)
            gpre[r, mine_u] = (grad_hidden * (pre_gate * sigma)).astype(BF16)

    def weight_grads(g):
        @pl.loop(3 * g, 3 * g + 3)
        def _(k):
            kr = rows_of(k, H)
            x = xg[g, :, pl.ds(pl.multiple_of((k - 3 * g) * H, H), H)]
            gg[kr, :] = lax.dot_general(x, gpre[:, mine_g], TN, preferred_element_type=F32).astype(BF16)
            gu[kr, :] = lax.dot_general(x, gpre[:, mine_u], TN, preferred_element_type=F32).astype(BF16)

        @pl.loop(2 * g, 2 * g + 2)
        def _(k):
            w = lax.dot_general(hid[:, mine_g], yd[k], TN, preferred_element_type=F32)
            gd[:, rows_of(k, RS)] = w.astype(BF16)

    def program(t):
        pending = []

        def send(src, dst, ss, rs, device):
            c = remote(src, dst, ss, rs, device)
            c.start()
            pending.append(c)

        if t == 1:
            slot_weight = jnp.sum(spread0 * w0_row + spread1 * w1_row, axis=1, keepdims=True)

        def dispatch(cols):
            v = jnp.dot(spread, cols, preferred_element_type=F32)
            return (v if t == 0 else slot_weight * v).astype(BF16)

        def exchange_x(g):
            if g:
                send_x[g] = dispatch(acts[g])
            xg[g, own_rows, :] = send_x[g, own_rows, :]
            for i, (dx, dy) in enumerate(partners):
                j = group_of(dx, dy)
                send(
                    send_x.at[g, rows_of(j, CAP), :], xg.at[g, own_rows, :],
                    d_send.at[g, i], d_recv.at[g, i], dev(j, yh, z, core),
                )

        def x_arrived(g):
            for i, (dx, dy) in enumerate(partners):
                src = rows_of(group_of(4 - dx, dy), CAP)
                arrived(xg.at[g, src, :], d_send.at[g, i], d_recv.at[g, i])
            send(xg.at[g], xg.at[g], dsib_send.at[g], dsib_recv.at[g], sibling)

        def sib_x(g):
            arrived(xg.at[g], dsib_send.at[g], dsib_recv.at[g])

        def exchange_y():
            for i, (dx, dy) in enumerate(partners):
                j = group_of(dx, dy)
                send(
                    send_y.at[rows_of(j, CAP), :], yd.at[z, own_rows, :],
                    a_send.at[i], a_recv.at[i], dev(j, yh, z, core),
                )

        def y_arrived():
            for i, (dx, dy) in enumerate(partners):
                src = rows_of(group_of(4 - dx, dy), CAP)
                arrived(yd.at[z, src, :], a_send.at[i], a_recv.at[i])

        def sib_y(*ds):
            for d in ds:
                for p in range(NP):
                    arrived(yd_view(zmod(z + d), p), sib_send.at[d % NZ, p], sib_recv.at[d % NZ, p])

        def gather():
            for s in range(5):
                for p in range(NP):
                    for way, nxt, sign in ((0, up, -1), (1, down, 1)):
                        split = (p < NP // 2) == (way == 0)
                        if s == 4 and not split:
                            continue
                        ref = yd_view(zmod(z + sign * s), p)
                        if s > 0:
                            arrived(ref, ring_send.at[way, s - 1, p], ring_recv.at[way, s - 1, p])
                        if s < 3 or (s == 3 and split):
                            send(ref, ref, ring_send.at[way, s, p], ring_recv.at[way, s, p], nxt)
                        if s > 0 or way == 0:
                            d = (sign * s) % NZ
                            send(ref, ref, sib_send.at[d, p], sib_recv.at[d, p], sibling)
                yield

        def spread_out(view, sems):
            s_send, s_recv, b_send, b_recv = sems

            def at(dz):
                return dev(e, yh, zmod(z + dz), core)

            def pass_on(d, h=None):
                ref = view(t, zmod(z + d), h)
                k = d % NZ if h != 1 else NZ
                send(ref, ref, b_send.at[k], b_recv.at[k], sibling)

            def got(i, d, h=None):
                arrived(view(t, zmod(z + d), h), s_send.at[i], s_recv.at[i])

            def give(i, d, dz, h=None):
                ref = view(t, zmod(z + d), h)
                send(ref, ref, s_send.at[i], s_recv.at[i], at(dz))

            give(0, 0, 2)
            give(1, 0, -2)
            give(2, 0, 1)
            give(3, 0, -1)
            pass_on(0)
            yield
            got(0, -2)
            give(4, -2, 1)
            give(5, -2, 2, 0)
            got(1, 2)
            give(6, 2, -1)
            give(7, 2, -2, 1)
            pass_on(-2)
            pass_on(2)
            got(2, -1)
            pass_on(-1)
            got(3, 1)
            pass_on(1)
            yield
            got(4, -3)
            pass_on(-3)
            got(6, 3)
            pass_on(3)
            got(5, -4, 0)
            pass_on(4, 0)
            got(7, 4, 1)
            pass_on(4, 1)
            yield

        def term(zd):
            cols = rows_of(zd, RS)
            if t == 0:
                v = jnp.dot(hid[...], wd[:, cols], preferred_element_type=F32)
            else:
                v = lax.dot_general(gpre[...], wgu[cols, :], NT, preferred_element_type=F32)
            for q in range(NQ):
                part[q, zd] = v[:, q * QC : (q + 1) * QC].astype(BF16)

        def other_terms():
            @pl.loop(0, 5)
            def _(i):
                term(zmod(z + 6 + i))

        probs = []

        def back(q):
            def rs_start(way, s, h):
                send(
                    part.at[q, target(way, s), half(h), :], land[way].at[q, s, half(h), :],
                    rs_send.at[q, way * 4 + s, h], rs_recv.at[q, way * 4 + s, h], up if way == 0 else down,
                )

            def rs_arrived(way, s, h):
                arrived(land[way].at[q, s, half(h), :], rs_send.at[q, way * 4 + s, h], rs_recv.at[q, way * 4 + s, h])

            def rs_add(way, s, h):
                zd = target(way, s + 1)
                part[q, zd, half(h), :] = (
                    part[q, zd, half(h), :].astype(F32) + land[way][q, s, half(h), :].astype(F32)
                ).astype(BF16)

            if q == 0:
                term(zmod(z + 4))
            rs_start(0, 0, 0)
            rs_start(1, 0, 1)
            if q == 0:
                term(zmod(z + 3))
            rs_start(0, 1, 1)
            if q == 0:
                term(zmod(z + 5))
            rs_start(1, 1, 0)
            yield
            for way, h in ((0, 0), (1, 1)):
                rs_arrived(way, 0, h)
                rs_add(way, 0, h)
                rs_start(way, 1, h)
            yield
            for s in (1, 2):
                for way, h in ((0, 1), (1, 0), (0, 0), (1, 1)):
                    rs_arrived(way, s, h)
                    rs_add(way, s, h)
                    rs_start(way, s + 1, h)
                yield
            for h in range(2):
                for way in range(2):
                    rs_arrived(way, 3, h)
                part[q, z, half(h), :] = (
                    part[q, z, half(h), :].astype(F32)
                    + rp[q, 3, half(h), :].astype(F32)
                    + rm[q, 3, half(h), :].astype(F32)
                ).astype(BF16)
            rc[q, yh, own_rows, :] = part[q, z, own_rows, :]
            for i in range(E):
                for dy in range(2):
                    if i or dy:
                        b = lax.rem(e + i, E)
                        send(
                            part.at[q, z, rows_of(b, CAP), :], rc.at[q, yh, own_rows, :],
                            c_send.at[q, i * 2 + dy], c_recv.at[q, i * 2 + dy],
                            dev(b, lax.rem(yh + dy, 2), z, core),
                        )
            yield
            for i in range(E):
                for dy in range(2):
                    if i or dy:
                        src = rows_of(lax.rem(e + E - i, E), CAP)
                        arrived(
                            rc.at[q, lax.rem(yh + dy, 2), src, :],
                            c_send.at[q, i * 2 + dy], c_recv.at[q, i * 2 + dy],
                        )
            summed = (rc[q, 0].astype(F32) + rc[q, 1].astype(F32)).astype(BF16)
            out0 = jnp.dot(pick0, summed, preferred_element_type=F32)
            out1 = jnp.dot(pick1, summed, preferred_element_type=F32)
            mixed = w0 * out0 + w1 * out1 if t == 0 else out0 + out1
            outs[t, q, z] = mixed.astype(BF16)

            def view(kind, zz, h=None):
                rows = slice(0, TOK) if h is None else slice(h * (TOK // 2), (h + 1) * (TOK // 2))
                return outs.at[kind, q, zz, rows, :]

            sems = (o_send.at[q], o_recv.at[q], osib_send.at[q], osib_recv.at[q])
            steps = spread_out(view, sems)
            next(steps)
            if t == 0:
                cot = cot_part[:, q * QC : (q + 1) * QC].astype(F32)
                probs.append((jnp.sum(cot * out0, axis=1, keepdims=True), jnp.sum(cot * out1, axis=1, keepdims=True)))
                if q == NQ - 1:
                    p0 = sum(v[0] for v in probs)
                    p1 = sum(v[1] for v in probs)
                    gp[z] = (jnp.where(lane == 0, p0, 0.0) + jnp.where(lane == 1, p1, 0.0)).T[0:8, :]
                    for dz in range(1, NZ):
                        send(gp.at[z], gp.at[z], g_send.at[dz], g_recv.at[dz], dev(e, yh, lax.rem(z + dz, NZ), core))
            yield
            for _ in steps:
                yield
            for k in range(NZ + 1):
                h = None if k not in (4, NZ) else k // NZ
                arrived(view(1 - t, zmod(z + (4 if k == NZ else k)), h), osib_send.at[q, k], osib_recv.at[q, k])
            yield

        if t == 0:
            load_x[0].wait()
            send_x[0] = dispatch(acts[0])
        else:
            own_c.wait()
            send_y[...] = dispatch(cot_part[...])
            yd[z, own_rows, :] = send_y[own_rows, :]
        pl.semaphore_wait(barrier, 2 * E - 1 + NZ)
        if t == 0:
            for g in range(NG):
                if g:
                    load_x[g].wait()
                exchange_x(g)
            send(w_gate.at[0], wgu.at[:, 0:H], wpre_sem.at[0], wpre_sem.at[2], sibling)
            send(w_up.at[0], wgu.at[:, 2 * H : 3 * H], wpre_sem.at[1], wpre_sem.at[3], sibling)
        else:
            exchange_y()
            send(w_down.at[0], wd.at[H : 2 * H, :], wpre_sem.at[0], wpre_sem.at[2], sibling)
        acc_gu[...] = jnp.zeros_like(acc_gu)
        acc_h[...] = jnp.zeros_like(acc_h)
        pick0 = spread0.T.astype(BF16)
        pick1 = spread1.T.astype(BF16)
        if t == 0:
            w0 = jnp.broadcast_to(w0_row, (TOK, TOK)).T[:, 0:1]
            w1 = jnp.broadcast_to(w1_row, (TOK, TOK)).T[:, 0:1]
            own_c.wait()
        for c in (own_g, own_u, own_d):
            c.wait()
        ring = gather()
        q0, q1, q2 = (back(q) for q in range(NQ))

        def go(*order):
            for q in order:
                next(q)

        if t == 0:
            x_arrived(0)
            add_x(0)
            sib_y(0)
            add_y(z)
            x_arrived(1)
            add_x(1)
            sib_y(1, -1)
            add_pair(1)
            x_arrived(2)
            add_x(2)
            sib_y(2, -2)
            add_pair(2)
            x_arrived(3)
            add_x(3)
            forward()
            sib_y(3, -3)
            add_pair(3)
            sib_y(4)
            add_y(zmod(z + 4))
            backward()
            send(gpre.at[:, 0:H], gpre.at[:, 0:H], act_sem.at[0], act_sem.at[2], sibling)
            send(gpre.at[:, 2 * H : 3 * H], gpre.at[:, 2 * H : 3 * H], act_sem.at[1], act_sem.at[3], sibling)
            arrived(wd.at[H : 2 * H, :], wpre_sem.at[0], wpre_sem.at[2])
            arrived(hid.at[:, H : 2 * H], act_sem.at[0], act_sem.at[2])
        else:
            y_arrived()
            go(ring)
            add_y(z)
            go(ring)
            add_pair(1)
            sib_x(0)
            add_x(0)
            go(ring)
            add_pair(2)
            sib_x(1)
            add_x(1)
            go(ring)
            add_pair(3)
            sib_x(2)
            add_x(2)
            go(ring)
            add_y(zmod(z + 4))
            sib_x(3)
            add_x(3)
            forward()
            send(hid.at[:, H : 2 * H], hid.at[:, H : 2 * H], act_sem.at[0], act_sem.at[2], sibling)
            backward()
            arrived(wgu.at[:, 0:H], wpre_sem.at[0], wpre_sem.at[2])
            arrived(wgu.at[:, 2 * H : 3 * H], wpre_sem.at[1], wpre_sem.at[3])
            arrived(gpre.at[:, 0:H], act_sem.at[0], act_sem.at[2])
            arrived(gpre.at[:, 2 * H : 3 * H], act_sem.at[1], act_sem.at[3])
        go(q0, q1)
        other_terms()
        go(q0, q2)
        weight_grads(0)
        go(q0, q1)
        weight_grads(1)
        go(q0, q1, q2)
        weight_grads(2)
        go(q0, q1, q2)
        weight_grads(3)
        go(q1, q2)
        go(q0)
        go(q2)
        go(q1, q0)
        go(q0, q1)
        go(q2)
        go(q1)
        go(q2)
        go(q2)
        if t == 0:
            for dz in range(1, NZ):
                arrived(gp.at[zmod(z - dz)], g_send.at[dz], g_recv.at[dz])
            total = gp[0]
            for zz in range(1, NZ):
                total = total + gp[zz]
            gp_sum[...] = total
            send(gp_sum, gp_sum, gsum_sem.at[0], gsum_sem.at[1], sibling)
        else:
            arrived(gp_sum, gsum_sem.at[0], gsum_sem.at[1])
        go(q0, q1, q2)

        for q in (ring, q0, q1, q2):
            assert (t == 0 and q is ring) or next(q, None) is None
        prob[...] = gp_sum[0:2, :]
        for c in pending:
            c.wait_send()

    for c in range(2):

        @pl.when(core == c)
        def _(c=c):
            program(c)


def store(outs, prob, gg, gu, gd, moe_out, grad_tokens, grad_prob, grad_gate, grad_up, grad_down, sem):
    copies = []

    def copy(src, dst, i):
        c = pltpu.make_async_copy(src, dst, sem.at[i])
        c.start()
        copies.append(c)

    for kind, dst in enumerate((moe_out, grad_tokens)):
        for q in range(NQ):
            for zz in range(NZ):
                columns = slice(zz * RS + q * QC, zz * RS + (q + 1) * QC)
                copy(outs.at[kind, q, zz], dst.at[:, columns], (kind * NQ + q) * NZ + zz)
    first = 2 * NQ * NZ
    copy(gg, grad_gate.at[0], first)
    copy(gu, grad_up.at[0], first + 1)
    copy(gd, grad_down.at[0], first + 2)
    copy(prob, grad_prob, first + 3)
    for c in copies:
        c.wait()


def per_device(tokens, assignment, route_weight, cotangent, w_gate, w_up, w_down):
    hbm = pl.BlockSpec(memory_space=pl.ANY)
    vmem = pl.BlockSpec(memory_space=pltpu.VMEM)
    dma = pltpu.SemaphoreType.DMA
    held = pl.pallas_call(
        kernel,
        out_shape=(
            pltpu.VMEM((2, NQ, NZ, TOK, QC), BF16),
            pltpu.VMEM((2, TOK), F32),
            pltpu.VMEM((D, H), BF16),
            pltpu.VMEM((D, H), BF16),
            pltpu.VMEM((H, D), BF16),
        ),
        in_specs=[hbm, vmem, vmem, hbm, hbm, hbm, hbm],
        out_specs=(vmem,) * 5,
        scratch_shapes=[
            pltpu.VMEM((NG, TOK, KG), BF16),
            pltpu.VMEM((TOK, RS), BF16),
            pltpu.VMEM((D, 4 * H), BF16),
            pltpu.VMEM((2 * H, D), BF16),
            pltpu.VMEM((NG, SLOTS, KG), BF16),
            pltpu.VMEM((SLOTS, RS), BF16),
            pltpu.VMEM((NG, SLOTS, KG), BF16),
            pltpu.VMEM((NZ, SLOTS, RS), BF16),
            pltpu.VMEM((SLOTS, 2 * H), F32),
            pltpu.VMEM((SLOTS, H), F32),
            pltpu.VMEM((SLOTS, 2 * H), BF16),
            pltpu.VMEM((SLOTS, 4 * H), BF16),
            pltpu.VMEM((NQ, NZ, SLOTS, QC), BF16),
            pltpu.VMEM((NQ, 4, SLOTS, QC), BF16),
            pltpu.VMEM((NQ, 4, SLOTS, QC), BF16),
            pltpu.VMEM((NQ, 2, SLOTS, QC), BF16),
            pltpu.VMEM((NZ, 8, TOK), F32),
            pltpu.VMEM((8, TOK), F32),
            dma((5 + NG,)), dma((4,)),
            dma((E - 1,)), dma((E - 1,)), dma((NG, E - 1)), dma((NG, E - 1)),
            dma((2, 4, NP)), dma((2, 4, NP)), dma((NZ, NP)), dma((NZ, NP)), dma((NG,)), dma((NG,)),
            dma((4,)), dma((NQ, 8, 2)), dma((NQ, 8, 2)), dma((NQ, 2 * E)), dma((NQ, 2 * E)),
            dma((NQ, 8)), dma((NQ, 8)), dma((NQ, NZ + 1)), dma((NQ, NZ + 1)),
            dma((NZ,)), dma((NZ,)), dma((2,)),
        ],
        compiler_params=pltpu.CompilerParams(
            collective_id=0, has_side_effects=True, vmem_limit_bytes=50 * 1024 * 1024
        ),
    )(tokens, assignment.T, route_weight.T, cotangent, w_gate, w_up, w_down)
    moe_out, grad_tokens, grad_prob, grad_gate, grad_up, grad_down = pl.pallas_call(
        store,
        out_shape=(
            jax.ShapeDtypeStruct((TOK, D), BF16),
            jax.ShapeDtypeStruct((TOK, D), BF16),
            jax.ShapeDtypeStruct((2, TOK), F32),
            jax.ShapeDtypeStruct((1, D, H), BF16),
            jax.ShapeDtypeStruct((1, D, H), BF16),
            jax.ShapeDtypeStruct((1, H, D), BF16),
        ),
        in_specs=[vmem] * 5,
        out_specs=(hbm,) * 6,
        scratch_shapes=[dma((2 * NQ * NZ + 4,))],
        compiler_params=pltpu.CompilerParams(vmem_limit_bytes=16 * 1024 * 1024),
    )(*held)
    return (moe_out, grad_tokens, grad_prob.T, grad_gate, grad_up, grad_down)


def solution(mesh):
    return jax.shard_map(
        per_device,
        mesh=mesh,
        in_specs=(
            P("expert", None),
            P("expert", None),
            P("expert", None),
            P("expert", None),
            P("expert", None, "fsdp"),
            P("expert", None, "fsdp"),
            P("expert", "fsdp", None),
        ),
        out_specs=(
            P("expert", None),
            P("expert", None),
            P("expert", None),
            P("expert", None, "fsdp"),
            P("expert", None, "fsdp"),
            P("expert", "fsdp", None),
        ),
        check_vma=False,
    )
```

```python
import jax
import jax.numpy as jnp
from jax import lax
from jax.experimental import pallas as pl
from jax.experimental.pallas import tpu as pltpu
from jax.sharding import PartitionSpec as P

MESH = pl.DeviceIdType.MESH
BF16 = jnp.bfloat16
F32 = jnp.float32
NT = (((1,), (1,)), ((), ()))
TN = (((0,), (0,)), ((), ()))

E = 8
NZ = 8
CAP = 48
TOK = 128
SLOTS = E * CAP
D = 3072
H = 256
HALF = SLOTS // 2
NG = 4
KG = D // NG
RS = D // NZ
QC = 128
NQ = RS // QC
NP = 4


def rows_of(index, size):
    return pl.ds(pl.multiple_of(index * size, size), size)


def kernel(
    tokens, assign_t, weight_t, cotangent, w_gate, w_up, w_down,
    outs, prob, gg, gu, gd,
    acts, cot_part, wgu, wd, send_x, send_y, xg, yd, acc_gu, acc_h, hid, gpre,
    part, rp, rm, rc, yx, gp, gp_sum,
    load_sem, wpre_sem,
    a_send, a_recv, d_send, d_recv, ring_send, ring_recv, sib_send, sib_recv, dsib_send, dsib_recv,
    act_sem, yx_send, yx_recv, rs_send, rs_recv, c_send, c_recv, o_send, o_recv, osib_send, osib_recv, g_send, g_recv, gsum_sem,
):
    e = lax.axis_index("expert")
    f = lax.axis_index("fsdp")
    core = lax.rem(f, 2)
    z = lax.rem(lax.div(f, 2), NZ)
    yh = lax.div(f, 2 * NZ)

    def dev(e_, yh_, z_, c_):
        return (e_, yh_ * (2 * NZ) + z_ * 2 + c_)

    sibling = dev(e, yh, z, 1 - core)
    up = dev(e, yh, lax.rem(z + 1, NZ), core)
    down = dev(e, yh, lax.rem(z + NZ - 1, NZ), core)

    def zmod(v):
        return lax.rem(v + 2 * NZ, NZ)

    def remote(src, dst, ss, rs, device):
        return pltpu.make_async_remote_copy(
            src_ref=src, dst_ref=dst, send_sem=ss, recv_sem=rs, device_id=device, device_id_type=MESH
        )

    def arrived(dst, ss, rs):
        remote(dst, dst, ss, rs, sibling).wait_recv()

    load_x = [
        pltpu.make_async_copy(tokens.at[:, g * KG : (g + 1) * KG], acts.at[g], load_sem.at[5 + g]) for g in range(NG)
    ]
    own_c = pltpu.make_async_copy(cotangent.at[:, rows_of(z, RS)], cot_part, load_sem.at[4])
    own_c.start()

    @pl.when(core == 0)
    def _():
        for c in load_x:
            c.start()

    own_g = pltpu.make_async_copy(w_gate.at[0], wgu.at[:, rows_of(core, H)], load_sem.at[1])
    own_u = pltpu.make_async_copy(w_up.at[0], wgu.at[:, rows_of(core + 2, H)], load_sem.at[2])
    own_d = pltpu.make_async_copy(w_down.at[0], wd.at[rows_of(core, H), :], load_sem.at[3])
    for c in (own_g, own_u, own_d):
        c.start()

    barrier = pltpu.get_barrier_semaphore()

    def greet(device):
        pl.semaphore_signal(barrier, inc=1, device_id=device, device_id_type=MESH)

    greet(sibling)
    for i in range(E):
        for dy in range(2):
            if i or dy:
                greet(dev(lax.rem(e + i, E), lax.rem(yh + dy, 2), z, core))
    for dz in range(1, NZ):
        greet(dev(e, yh, lax.rem(z + dz, NZ), core))

    a0 = assign_t[0:1, :]
    a1 = assign_t[1:2, :]
    w0_row = weight_t[0:1, :]
    w1_row = weight_t[1:2, :]
    expert = lax.broadcasted_iota(jnp.int32, (8, TOK), 0)
    hot0 = (expert == a0).astype(F32)
    hot1 = (expert == a1).astype(F32)
    lane = lax.broadcasted_iota(jnp.int32, (TOK, TOK), 1)
    row = lax.broadcasted_iota(jnp.int32, (TOK, TOK), 0)
    before = (row < lane).astype(BF16)
    count = jnp.dot((hot0 + hot1).astype(BF16), before, preferred_element_type=F32)
    slot0 = a0 * CAP + jnp.sum(hot0 * count, axis=0, keepdims=True).astype(jnp.int32)
    slot1 = a1 * CAP + jnp.sum(hot1 * count, axis=0, keepdims=True).astype(jnp.int32)
    slot = lax.broadcasted_iota(jnp.int32, (SLOTS, TOK), 0)
    spread0 = (slot == slot0).astype(F32)
    spread1 = (slot == slot1).astype(F32)
    spread = (spread0 + spread1).astype(BF16)
    own_rows = rows_of(e, CAP)
    mine_g = rows_of(core, H)
    mine_u = rows_of(core + 2, H)
    land = (rp, rm)

    def target(way, s):
        return zmod(z + 4 - s) if way == 0 else zmod(z - 4 + s)

    def yd_view(zz, p):
        return yd.at[zz, p * (SLOTS // NP) : (p + 1) * (SLOTS // NP), :]

    partners = ((1, 0), (3, 0), (0, 1), (2, 0), (1, 1), (3, 1), (2, 1))
    ey = lax.div(e, 4)
    ex = lax.rem(e, 4)

    def group_of(dx, dy):
        return lax.rem(ey + dy, 2) * 4 + lax.rem(ex + dx, 4)

    def add_x(g):
        kr = rows_of(g, KG)
        acc_gu[:, 0:H] += jnp.dot(xg[g], wgu[kr, mine_g], preferred_element_type=F32)
        acc_gu[:, H : 2 * H] += jnp.dot(xg[g], wgu[kr, mine_u], preferred_element_type=F32)

    def add_y(k):
        acc_h[...] += lax.dot_general(yd[k], wd[mine_g, rows_of(k, RS)], NT, preferred_element_type=F32)

    def add_pair(s):
        @pl.loop(0, 2)
        def _(i):
            add_y(zmod(z - s + 2 * s * i))

    def forward():
        @pl.loop(0, E)
        def _(b):
            r = rows_of(b, CAP)
            pre_gate = acc_gu[r, 0:H]
            hid[r, mine_g] = (pre_gate * jax.nn.sigmoid(pre_gate) * acc_gu[r, H : 2 * H]).astype(BF16)

    def backward():
        @pl.loop(0, E)
        def _(b):
            r = rows_of(b, CAP)
            pre_gate = acc_gu[r, 0:H]
            grad_hidden = acc_h[r, :]
            sigma = jax.nn.sigmoid(pre_gate)
            gpre[r, mine_g] = (
                grad_hidden * acc_gu[r, H : 2 * H] * sigma * (1.0 + pre_gate * (1.0 - sigma))
            ).astype(BF16)
            gpre[r, mine_u] = (grad_hidden * (pre_gate * sigma)).astype(BF16)

    def weight_grads(g):
        @pl.loop(3 * g, 3 * g + 3)
        def _(k):
            kr = rows_of(k, H)
            x = xg[g, :, pl.ds(pl.multiple_of((k - 3 * g) * H, H), H)]
            gg[kr, :] = lax.dot_general(x, gpre[:, mine_g], TN, preferred_element_type=F32).astype(BF16)
            gu[kr, :] = lax.dot_general(x, gpre[:, mine_u], TN, preferred_element_type=F32).astype(BF16)

        @pl.loop(2 * g, 2 * g + 2)
        def _(k):
            w = lax.dot_general(hid[:, mine_g], yd[k], TN, preferred_element_type=F32)
            gd[:, rows_of(k, RS)] = w.astype(BF16)

    def program(t):
        pending = []

        def send(src, dst, ss, rs, device):
            c = remote(src, dst, ss, rs, device)
            c.start()
            pending.append(c)

        if t == 1:
            slot_weight = jnp.sum(spread0 * w0_row + spread1 * w1_row, axis=1, keepdims=True)

        def dispatch(cols):
            v = jnp.dot(spread, cols, preferred_element_type=F32)
            return (v if t == 0 else slot_weight * v).astype(BF16)

        def exchange_x(g):
            if g:
                send_x[g] = dispatch(acts[g])
            xg[g, own_rows, :] = send_x[g, own_rows, :]
            for i, (dx, dy) in enumerate(partners):
                j = group_of(dx, dy)
                send(
                    send_x.at[g, rows_of(j, CAP), :], xg.at[g, own_rows, :],
                    d_send.at[g, i], d_recv.at[g, i], dev(j, yh, z, core),
                )

        def x_arrived(g):
            for i, (dx, dy) in enumerate(partners):
                src = rows_of(group_of(4 - dx, dy), CAP)
                arrived(xg.at[g, src, :], d_send.at[g, i], d_recv.at[g, i])
            send(xg.at[g], xg.at[g], dsib_send.at[g], dsib_recv.at[g], sibling)

        def sib_x(g):
            arrived(xg.at[g], dsib_send.at[g], dsib_recv.at[g])

        def exchange_y():
            for i, (dx, dy) in enumerate(partners):
                j = group_of(dx, dy)
                send(
                    send_y.at[rows_of(j, CAP), :], yd.at[z, own_rows, :],
                    a_send.at[i], a_recv.at[i], dev(j, yh, z, core),
                )

        def y_arrived():
            for i, (dx, dy) in enumerate(partners):
                src = rows_of(group_of(4 - dx, dy), CAP)
                arrived(yd.at[z, src, :], a_send.at[i], a_recv.at[i])

        def sib_y(*ds):
            for d in ds:
                for p in range(NP):
                    arrived(yd_view(zmod(z + d), p), sib_send.at[d % NZ, p], sib_recv.at[d % NZ, p])

        def gather():
            for s in range(5):
                for p in range(NP):
                    for way, nxt, sign in ((0, up, -1), (1, down, 1)):
                        split = (p < NP // 2) == (way == 0)
                        if s == 4 and not split:
                            continue
                        ref = yd_view(zmod(z + sign * s), p)
                        if s > 0:
                            arrived(ref, ring_send.at[way, s - 1, p], ring_recv.at[way, s - 1, p])
                        if s < 3 or (s == 3 and split):
                            send(ref, ref, ring_send.at[way, s, p], ring_recv.at[way, s, p], nxt)
                        if s > 0 or way == 0:
                            d = (sign * s) % NZ
                            send(ref, ref, sib_send.at[d, p], sib_recv.at[d, p], sibling)
                yield

        def spread_out(view, sems):
            s_send, s_recv, b_send, b_recv = sems

            def at(dz):
                return dev(e, yh, zmod(z + dz), core)

            def pass_on(d, h=None):
                ref = view(t, zmod(z + d), h)
                k = d % NZ if h != 1 else NZ
                send(ref, ref, b_send.at[k], b_recv.at[k], sibling)

            def got(i, d, h=None):
                arrived(view(t, zmod(z + d), h), s_send.at[i], s_recv.at[i])

            def give(i, d, dz, h=None):
                ref = view(t, zmod(z + d), h)
                send(ref, ref, s_send.at[i], s_recv.at[i], at(dz))

            give(0, 0, 2)
            give(1, 0, -2)
            give(2, 0, 1)
            give(3, 0, -1)
            pass_on(0)
            yield
            got(0, -2)
            give(4, -2, 1)
            give(5, -2, 2, 0)
            got(1, 2)
            give(6, 2, -1)
            give(7, 2, -2, 1)
            pass_on(-2)
            pass_on(2)
            got(2, -1)
            pass_on(-1)
            got(3, 1)
            pass_on(1)
            yield
            got(4, -3)
            pass_on(-3)
            got(6, 3)
            pass_on(3)
            got(5, -4, 0)
            pass_on(4, 0)
            got(7, 4, 1)
            pass_on(4, 1)
            yield

        def term(zd):
            cols = rows_of(zd, RS)
            if t == 0:
                v = jnp.dot(hid[...], wd[:, cols], preferred_element_type=F32)
            else:
                v = lax.dot_general(gpre[...], wgu[cols, :], NT, preferred_element_type=F32)
            for q in range(NQ):
                part[q, zd] = v[:, q * QC : (q + 1) * QC].astype(BF16)

        def other_terms():
            @pl.loop(0, 5)
            def _(i):
                term(zmod(z + 6 + i))

        probs = []

        def back(q):
            shared = q == NQ - 1

            def half(h):
                if shared:
                    return pl.ds(pl.multiple_of(yh * HALF + h * (HALF // 2), HALF // 2), HALF // 2)
                return slice(h * HALF, (h + 1) * HALF)

            def add_other(zd, d):
                if shared:
                    mine = rows_of(yh, HALF)
                    arrived(yx.at[zd], yx_send.at[d % NZ], yx_recv.at[d % NZ])
                    part[q, zd, mine, :] = (part[q, zd, mine, :].astype(F32) + yx[zd].astype(F32)).astype(BF16)

            def rs_start(way, s, h):
                send(
                    part.at[q, target(way, s), half(h), :], land[way].at[q, s, half(h), :],
                    rs_send.at[q, way * 4 + s, h], rs_recv.at[q, way * 4 + s, h], up if way == 0 else down,
                )

            def rs_arrived(way, s, h):
                arrived(land[way].at[q, s, half(h), :], rs_send.at[q, way * 4 + s, h], rs_recv.at[q, way * 4 + s, h])

            def rs_add(way, s, h):
                zd = target(way, s + 1)
                part[q, zd, half(h), :] = (
                    part[q, zd, half(h), :].astype(F32) + land[way][q, s, half(h), :].astype(F32)
                ).astype(BF16)

            if shared:
                for d in (4, 3, 5, 2, 6, 1, 7, 0):
                    zd = zmod(z + d)
                    send(
                        part.at[q, zd, rows_of(1 - yh, HALF), :], yx.at[zd],
                        yx_send.at[d], yx_recv.at[d], dev(e, 1 - yh, z, core),
                    )
                yield
            if q == 0:
                term(zmod(z + 4))
            add_other(zmod(z + 4), 4)
            rs_start(0, 0, 0)
            rs_start(1, 0, 1)
            if q == 0:
                term(zmod(z + 3))
            add_other(zmod(z + 3), 3)
            rs_start(0, 1, 1)
            if q == 0:
                term(zmod(z + 5))
            add_other(zmod(z + 5), 5)
            rs_start(1, 1, 0)
            yield
            for way, h in ((0, 0), (1, 1)):
                rs_arrived(way, 0, h)
                rs_add(way, 0, h)
                rs_start(way, 1, h)
            yield
            for s in (1, 2):
                add_other(zmod(z + 3 - s), 3 - s)
                add_other(zmod(z + 5 + s), 5 + s)
                for way, h in ((0, 1), (1, 0), (0, 0), (1, 1)):
                    rs_arrived(way, s, h)
                    rs_add(way, s, h)
                    rs_start(way, s + 1, h)
                yield
            add_other(z, 0)
            for h in range(2):
                for way in range(2):
                    rs_arrived(way, 3, h)
                part[q, z, half(h), :] = (
                    part[q, z, half(h), :].astype(F32)
                    + rp[q, 3, half(h), :].astype(F32)
                    + rm[q, 3, half(h), :].astype(F32)
                ).astype(BF16)
            if shared:
                def give(i, dy):
                    b = yh * 4 + lax.rem(ex + i, 4)
                    return remote(
                        part.at[q, z, rows_of(b, CAP), :], rc.at[q, 0, own_rows, :],
                        c_send.at[q, i * 2 + dy], c_recv.at[q, i * 2 + ey], dev(b, lax.rem(yh + dy, 2), z, core),
                    )

                @pl.when(yh == ey)
                def _():
                    rc[q, 0, own_rows, :] = part[q, z, own_rows, :]

                @pl.when(yh != ey)
                def _():
                    give(0, 0).start()

                for i in range(4):
                    for dy in range(2):
                        if i or dy:
                            c = give(i, dy)
                            c.start()
                            pending.append(c)
            else:
                rc[q, yh, own_rows, :] = part[q, z, own_rows, :]
                for i in range(E):
                    for dy in range(2):
                        if i or dy:
                            b = lax.rem(e + i, E)
                            send(
                                part.at[q, z, rows_of(b, CAP), :], rc.at[q, yh, own_rows, :],
                                c_send.at[q, i * 2 + dy], c_recv.at[q, i * 2 + dy],
                                dev(b, lax.rem(yh + dy, 2), z, core),
                            )
            yield
            if shared:
                for i in range(4):
                    for side in range(2):
                        src = rc.at[q, 0, rows_of(side * 4 + lax.rem(ex + 4 - i, 4), CAP), :]
                        if i:
                            arrived(src, c_send.at[q, i * 2 + side], c_recv.at[q, i * 2 + side])
                        else:

                            @pl.when(jnp.logical_or(yh != ey, ey != side))
                            def _(src=src, side=side):
                                arrived(src, c_send.at[q, side], c_recv.at[q, side])

                @pl.when(yh != ey)
                def _():
                    give(0, 0).wait_send()

                summed = rc[q, 0]
            else:
                for i in range(E):
                    for dy in range(2):
                        if i or dy:
                            src = rows_of(lax.rem(e + E - i, E), CAP)
                            arrived(
                                rc.at[q, lax.rem(yh + dy, 2), src, :],
                                c_send.at[q, i * 2 + dy], c_recv.at[q, i * 2 + dy],
                            )
                summed = (rc[q, 0].astype(F32) + rc[q, 1].astype(F32)).astype(BF16)
            out0 = jnp.dot(pick0, summed, preferred_element_type=F32)
            out1 = jnp.dot(pick1, summed, preferred_element_type=F32)
            mixed = w0 * out0 + w1 * out1 if t == 0 else out0 + out1
            outs[t, :, pl.ds(pl.multiple_of(z * RS + q * QC, QC), QC)] = mixed.astype(BF16)

            def columns(zz):
                return pl.ds(pl.multiple_of(zz * RS + q * QC, QC), QC)

            def view(kind, zz, h=None):
                rows = slice(0, TOK) if h is None else slice(h * (TOK // 2), (h + 1) * (TOK // 2))
                return outs.at[kind, rows, columns(zz)]

            sems = (o_send.at[q], o_recv.at[q], osib_send.at[q], osib_recv.at[q])
            steps = spread_out(view, sems)
            next(steps)
            if t == 0:
                cot = cot_part[:, q * QC : (q + 1) * QC].astype(F32)
                probs.append((jnp.sum(cot * out0, axis=1, keepdims=True), jnp.sum(cot * out1, axis=1, keepdims=True)))
                if q == NQ - 1:
                    p0 = sum(v[0] for v in probs)
                    p1 = sum(v[1] for v in probs)
                    gp[z] = (jnp.where(lane == 0, p0, 0.0) + jnp.where(lane == 1, p1, 0.0)).T[0:8, :]
                    for dz in range(1, NZ):
                        send(gp.at[z], gp.at[z], g_send.at[dz], g_recv.at[dz], dev(e, yh, lax.rem(z + dz, NZ), core))
            yield
            for _ in steps:
                yield
            for k in range(NZ + 1):
                h = None if k not in (4, NZ) else k // NZ
                arrived(view(1 - t, zmod(z + (4 if k == NZ else k)), h), osib_send.at[q, k], osib_recv.at[q, k])
            yield

        if t == 0:
            load_x[0].wait()
            send_x[0] = dispatch(acts[0])
        else:
            own_c.wait()
            send_y[...] = dispatch(cot_part[...])
            yd[z, own_rows, :] = send_y[own_rows, :]
        pl.semaphore_wait(barrier, 2 * E - 1 + NZ)
        if t == 0:
            for g in range(NG):
                if g:
                    load_x[g].wait()
                exchange_x(g)
            send(w_gate.at[0], wgu.at[:, 0:H], wpre_sem.at[0], wpre_sem.at[2], sibling)
            send(w_up.at[0], wgu.at[:, 2 * H : 3 * H], wpre_sem.at[1], wpre_sem.at[3], sibling)
        else:
            exchange_y()
            send(w_down.at[0], wd.at[H : 2 * H, :], wpre_sem.at[0], wpre_sem.at[2], sibling)
        acc_gu[...] = jnp.zeros_like(acc_gu)
        acc_h[...] = jnp.zeros_like(acc_h)
        pick0 = spread0.T.astype(BF16)
        pick1 = spread1.T.astype(BF16)
        if t == 0:
            w0 = jnp.broadcast_to(w0_row, (TOK, TOK)).T[:, 0:1]
            w1 = jnp.broadcast_to(w1_row, (TOK, TOK)).T[:, 0:1]
            own_c.wait()
        for c in (own_g, own_u, own_d):
            c.wait()
        ring = gather()
        q0, q1, q2 = (back(q) for q in range(NQ))

        def go(*order):
            for q in order:
                next(q)

        if t == 0:
            x_arrived(0)
            add_x(0)
            sib_y(0)
            add_y(z)
            x_arrived(1)
            add_x(1)
            sib_y(1, -1)
            add_pair(1)
            x_arrived(2)
            add_x(2)
            sib_y(2, -2)
            add_pair(2)
            x_arrived(3)
            add_x(3)
            forward()
            sib_y(3, -3)
            add_pair(3)
            sib_y(4)
            add_y(zmod(z + 4))
            backward()
            send(gpre.at[:, 0:H], gpre.at[:, 0:H], act_sem.at[0], act_sem.at[2], sibling)
            send(gpre.at[:, 2 * H : 3 * H], gpre.at[:, 2 * H : 3 * H], act_sem.at[1], act_sem.at[3], sibling)
            arrived(wd.at[H : 2 * H, :], wpre_sem.at[0], wpre_sem.at[2])
            arrived(hid.at[:, H : 2 * H], act_sem.at[0], act_sem.at[2])
        else:
            y_arrived()
            go(ring)
            add_y(z)
            go(ring)
            add_pair(1)
            sib_x(0)
            add_x(0)
            go(ring)
            add_pair(2)
            sib_x(1)
            add_x(1)
            go(ring)
            add_pair(3)
            sib_x(2)
            add_x(2)
            go(ring)
            add_y(zmod(z + 4))
            sib_x(3)
            add_x(3)
            forward()
            send(hid.at[:, H : 2 * H], hid.at[:, H : 2 * H], act_sem.at[0], act_sem.at[2], sibling)
            backward()
            arrived(wgu.at[:, 0:H], wpre_sem.at[0], wpre_sem.at[2])
            arrived(wgu.at[:, 2 * H : 3 * H], wpre_sem.at[1], wpre_sem.at[3])
            arrived(gpre.at[:, 0:H], act_sem.at[0], act_sem.at[2])
            arrived(gpre.at[:, 2 * H : 3 * H], act_sem.at[1], act_sem.at[3])
        go(q0, q1)
        other_terms()
        go(q2, q0, q1)
        weight_grads(0)
        go(q0, q1, q2)
        weight_grads(1)
        go(q0, q1, q2, q0, q2, q1, q2, q0, q2)
        weight_grads(2)
        go(q1, q0, q2)
        weight_grads(3)
        go(q1, q2, q0, q1)
        if t == 0:
            for dz in range(1, NZ):
                arrived(gp.at[zmod(z - dz)], g_send.at[dz], g_recv.at[dz])
            total = gp[0]
            for zz in range(1, NZ):
                total = total + gp[zz]
            gp_sum[...] = total
            send(gp_sum, gp_sum, gsum_sem.at[0], gsum_sem.at[1], sibling)
        go(q2)
        if t == 1:
            arrived(gp_sum, gsum_sem.at[0], gsum_sem.at[1])
        go(q0, q1, q2)

        for q in (ring, q0, q1, q2):
            assert (t == 0 and q is ring) or next(q, None) is None
        prob[...] = gp_sum[0:2, :]
        for c in pending:
            c.wait_send()

    for c in range(2):

        @pl.when(core == c)
        def _(c=c):
            program(c)


def store(outs, prob, gg, gu, gd, moe_out, grad_tokens, grad_prob, grad_gate, grad_up, grad_down, sem):
    copies = []
    for i, (src, dst) in enumerate((
        (gg, grad_gate.at[0]), (gu, grad_up.at[0]), (gd, grad_down.at[0]),
        (outs.at[0], moe_out), (outs.at[1], grad_tokens), (prob, grad_prob),
    )):
        copies.append(pltpu.make_async_copy(src, dst, sem.at[i]))
    for c in copies:
        c.start()
    for c in copies:
        c.wait()


def per_device(tokens, assignment, route_weight, cotangent, w_gate, w_up, w_down):
    hbm = pl.BlockSpec(memory_space=pl.ANY)
    vmem = pl.BlockSpec(memory_space=pltpu.VMEM)
    dma = pltpu.SemaphoreType.DMA
    held = pl.pallas_call(
        kernel,
        out_shape=(
            pltpu.VMEM((2, TOK, D), BF16),
            pltpu.VMEM((2, TOK), F32),
            pltpu.VMEM((D, H), BF16),
            pltpu.VMEM((D, H), BF16),
            pltpu.VMEM((H, D), BF16),
        ),
        in_specs=[hbm, vmem, vmem, hbm, hbm, hbm, hbm],
        out_specs=(vmem,) * 5,
        scratch_shapes=[
            pltpu.VMEM((NG, TOK, KG), BF16),
            pltpu.VMEM((TOK, RS), BF16),
            pltpu.VMEM((D, 4 * H), BF16),
            pltpu.VMEM((2 * H, D), BF16),
            pltpu.VMEM((NG, SLOTS, KG), BF16),
            pltpu.VMEM((SLOTS, RS), BF16),
            pltpu.VMEM((NG, SLOTS, KG), BF16),
            pltpu.VMEM((NZ, SLOTS, RS), BF16),
            pltpu.VMEM((SLOTS, 2 * H), F32),
            pltpu.VMEM((SLOTS, H), F32),
            pltpu.VMEM((SLOTS, 2 * H), BF16),
            pltpu.VMEM((SLOTS, 4 * H), BF16),
            pltpu.VMEM((NQ, NZ, SLOTS, QC), BF16),
            pltpu.VMEM((NQ, 4, SLOTS, QC), BF16),
            pltpu.VMEM((NQ, 4, SLOTS, QC), BF16),
            pltpu.VMEM((NQ, 2, SLOTS, QC), BF16),
            pltpu.VMEM((NZ, HALF, QC), BF16),
            pltpu.VMEM((NZ, 8, TOK), F32),
            pltpu.VMEM((8, TOK), F32),
            dma((5 + NG,)), dma((4,)),
            dma((E - 1,)), dma((E - 1,)), dma((NG, E - 1)), dma((NG, E - 1)),
            dma((2, 4, NP)), dma((2, 4, NP)), dma((NZ, NP)), dma((NZ, NP)), dma((NG,)), dma((NG,)),
            dma((4,)), dma((NZ,)), dma((NZ,)), dma((NQ, 8, 2)), dma((NQ, 8, 2)), dma((NQ, 2 * E)), dma((NQ, 2 * E)),
            dma((NQ, 8)), dma((NQ, 8)), dma((NQ, NZ + 1)), dma((NQ, NZ + 1)),
            dma((NZ,)), dma((NZ,)), dma((2,)),
        ],
        compiler_params=pltpu.CompilerParams(
            collective_id=0, has_side_effects=True, vmem_limit_bytes=50 * 1024 * 1024
        ),
    )(tokens, assignment.T, route_weight.T, cotangent, w_gate, w_up, w_down)
    moe_out, grad_tokens, grad_prob, grad_gate, grad_up, grad_down = pl.pallas_call(
        store,
        out_shape=(
            jax.ShapeDtypeStruct((TOK, D), BF16),
            jax.ShapeDtypeStruct((TOK, D), BF16),
            jax.ShapeDtypeStruct((2, TOK), F32),
            jax.ShapeDtypeStruct((1, D, H), BF16),
            jax.ShapeDtypeStruct((1, D, H), BF16),
            jax.ShapeDtypeStruct((1, H, D), BF16),
        ),
        in_specs=[vmem] * 5,
        out_specs=(hbm,) * 6,
        scratch_shapes=[dma((6,))],
        compiler_params=pltpu.CompilerParams(vmem_limit_bytes=16 * 1024 * 1024),
    )(*held)
    return (moe_out, grad_tokens, grad_prob.T, grad_gate, grad_up, grad_down)


def solution(mesh):
    return jax.shard_map(
        per_device,
        mesh=mesh,
        in_specs=(
            P("expert", None),
            P("expert", None),
            P("expert", None),
            P("expert", None),
            P("expert", None, "fsdp"),
            P("expert", None, "fsdp"),
            P("expert", "fsdp", None),
        ),
        out_specs=(
            P("expert", None),
            P("expert", None),
            P("expert", None),
            P("expert", None, "fsdp"),
            P("expert", None, "fsdp"),
            P("expert", "fsdp", None),
        ),
        check_vma=False,
    )
```

```python
import jax
import jax.numpy as jnp
from jax import lax
from jax.experimental import pallas as pl
from jax.experimental.pallas import tpu as pltpu
from jax.sharding import PartitionSpec as P

MESH = pl.DeviceIdType.MESH
BF16 = jnp.bfloat16
F32 = jnp.float32
NT = (((1,), (1,)), ((), ()))
TN = (((0,), (0,)), ((), ()))

E = 8
NZ = 8
CAP = 48
TOK = 128
SLOTS = E * CAP
D = 3072
H = 256
HALF = SLOTS // 2
NG = 4
KG = D // NG
RS = D // NZ
QC = 128
NQ = RS // QC
NP = 4


def rows_of(index, size):
    return pl.ds(pl.multiple_of(index * size, size), size)


def kernel(
    tokens, assign_t, weight_t, cotangent, w_gate, w_up, w_down,
    outs, prob, gg, gu, gd,
    acts, cot_part, wgu, wd, send_x, send_y, xg, yd, acc_gu, acc_h, hid, gpre,
    part, rp, rm, rc, yx, gp, gp_sum,
    load_sem, wpre_sem,
    a_send, a_recv, d_send, d_recv, ring_send, ring_recv, sib_send, sib_recv, dsib_send, dsib_recv,
    act_sem, yx_send, yx_recv, rs_send, rs_recv, c_send, c_recv, o_send, o_recv, osib_send, osib_recv, g_send, g_recv, gsum_sem,
):
    e = lax.axis_index("expert")
    f = lax.axis_index("fsdp")
    core = lax.rem(f, 2)
    z = lax.rem(lax.div(f, 2), NZ)
    yh = lax.div(f, 2 * NZ)

    def dev(e_, yh_, z_, c_):
        return (e_, yh_ * (2 * NZ) + z_ * 2 + c_)

    sibling = dev(e, yh, z, 1 - core)
    up = dev(e, yh, lax.rem(z + 1, NZ), core)
    down = dev(e, yh, lax.rem(z + NZ - 1, NZ), core)

    def zmod(v):
        return lax.rem(v + 2 * NZ, NZ)

    def remote(src, dst, ss, rs, device):
        return pltpu.make_async_remote_copy(
            src_ref=src, dst_ref=dst, send_sem=ss, recv_sem=rs, device_id=device, device_id_type=MESH
        )

    def arrived(dst, ss, rs):
        remote(dst, dst, ss, rs, sibling).wait_recv()

    load_x = [
        pltpu.make_async_copy(tokens.at[:, g * KG : (g + 1) * KG], acts.at[g], load_sem.at[5 + g]) for g in range(NG)
    ]
    own_c = pltpu.make_async_copy(cotangent.at[:, rows_of(z, RS)], cot_part, load_sem.at[4])
    own_c.start()

    @pl.when(core == 0)
    def _():
        for c in load_x:
            c.start()

    own_g = pltpu.make_async_copy(w_gate.at[0], wgu.at[:, rows_of(core, H)], load_sem.at[1])
    own_u = pltpu.make_async_copy(w_up.at[0], wgu.at[:, rows_of(core + 2, H)], load_sem.at[2])
    own_d = pltpu.make_async_copy(w_down.at[0], wd.at[rows_of(core, H), :], load_sem.at[3])
    for c in (own_g, own_u, own_d):
        c.start()

    barrier = pltpu.get_barrier_semaphore()

    def greet(device):
        pl.semaphore_signal(barrier, inc=1, device_id=device, device_id_type=MESH)

    greet(sibling)
    for i in range(E):
        for dy in range(2):
            if i or dy:
                greet(dev(lax.rem(e + i, E), lax.rem(yh + dy, 2), z, core))
    for dz in range(1, NZ):
        greet(dev(e, yh, lax.rem(z + dz, NZ), core))

    a0 = assign_t[0:1, :]
    a1 = assign_t[1:2, :]
    w0_row = weight_t[0:1, :]
    w1_row = weight_t[1:2, :]
    expert = lax.broadcasted_iota(jnp.int32, (8, TOK), 0)
    hot0 = (expert == a0).astype(F32)
    hot1 = (expert == a1).astype(F32)
    lane = lax.broadcasted_iota(jnp.int32, (TOK, TOK), 1)
    row = lax.broadcasted_iota(jnp.int32, (TOK, TOK), 0)
    before = (row < lane).astype(BF16)
    count = jnp.dot((hot0 + hot1).astype(BF16), before, preferred_element_type=F32)
    slot0 = a0 * CAP + jnp.sum(hot0 * count, axis=0, keepdims=True).astype(jnp.int32)
    slot1 = a1 * CAP + jnp.sum(hot1 * count, axis=0, keepdims=True).astype(jnp.int32)
    slot = lax.broadcasted_iota(jnp.int32, (SLOTS, TOK), 0)
    spread0 = (slot == slot0).astype(F32)
    spread1 = (slot == slot1).astype(F32)
    spread = (spread0 + spread1).astype(BF16)
    own_rows = rows_of(e, CAP)
    mine_g = rows_of(core, H)
    mine_u = rows_of(core + 2, H)
    land = (rp, rm)

    def target(way, s):
        return zmod(z + 4 - s) if way == 0 else zmod(z - 4 + s)

    def yd_view(zz, p):
        return yd.at[zz, p * (SLOTS // NP) : (p + 1) * (SLOTS // NP), :]

    partners = ((1, 0), (3, 0), (0, 1), (2, 0), (1, 1), (3, 1), (2, 1))
    ey = lax.div(e, 4)
    ex = lax.rem(e, 4)

    def group_of(dx, dy):
        return lax.rem(ey + dy, 2) * 4 + lax.rem(ex + dx, 4)

    def add_x(g):
        kr = rows_of(g, KG)
        acc_gu[:, 0:H] += jnp.dot(xg[g], wgu[kr, mine_g], preferred_element_type=F32)
        acc_gu[:, H : 2 * H] += jnp.dot(xg[g], wgu[kr, mine_u], preferred_element_type=F32)

    def add_y(k):
        acc_h[...] += lax.dot_general(yd[k], wd[mine_g, rows_of(k, RS)], NT, preferred_element_type=F32)

    def add_pair(s):
        @pl.loop(0, 2)
        def _(i):
            add_y(zmod(z - s + 2 * s * i))

    def forward():
        @pl.loop(0, E)
        def _(b):
            r = rows_of(b, CAP)
            pre_gate = acc_gu[r, 0:H]
            hid[r, mine_g] = (pre_gate * jax.nn.sigmoid(pre_gate) * acc_gu[r, H : 2 * H]).astype(BF16)

    def backward():
        @pl.loop(0, E)
        def _(b):
            r = rows_of(b, CAP)
            pre_gate = acc_gu[r, 0:H]
            grad_hidden = acc_h[r, :]
            sigma = jax.nn.sigmoid(pre_gate)
            gpre[r, mine_g] = (
                grad_hidden * acc_gu[r, H : 2 * H] * sigma * (1.0 + pre_gate * (1.0 - sigma))
            ).astype(BF16)
            gpre[r, mine_u] = (grad_hidden * (pre_gate * sigma)).astype(BF16)

    def weight_grads(g):
        @pl.loop(3 * g, 3 * g + 3)
        def _(k):
            kr = rows_of(k, H)
            x = xg[g, :, pl.ds(pl.multiple_of((k - 3 * g) * H, H), H)]
            gg[kr, :] = lax.dot_general(x, gpre[:, mine_g], TN, preferred_element_type=F32).astype(BF16)
            gu[kr, :] = lax.dot_general(x, gpre[:, mine_u], TN, preferred_element_type=F32).astype(BF16)

        @pl.loop(2 * g, 2 * g + 2)
        def _(k):
            w = lax.dot_general(hid[:, mine_g], yd[k], TN, preferred_element_type=F32)
            gd[:, rows_of(k, RS)] = w.astype(BF16)

    def program(t):
        pending = []

        def send(src, dst, ss, rs, device):
            c = remote(src, dst, ss, rs, device)
            c.start()
            pending.append(c)

        if t == 1:
            slot_weight = jnp.sum(spread0 * w0_row + spread1 * w1_row, axis=1, keepdims=True)

        def dispatch(cols):
            v = jnp.dot(spread, cols, preferred_element_type=F32)
            return (v if t == 0 else slot_weight * v).astype(BF16)

        def exchange_x(g):
            if g:
                send_x[g] = dispatch(acts[g])
            xg[g, own_rows, :] = send_x[g, own_rows, :]
            for i, (dx, dy) in enumerate(partners):
                j = group_of(dx, dy)
                send(
                    send_x.at[g, rows_of(j, CAP), :], xg.at[g, own_rows, :],
                    d_send.at[g, i], d_recv.at[g, i], dev(j, yh, z, core),
                )

        def x_arrived(g):
            for i, (dx, dy) in enumerate(partners):
                src = rows_of(group_of(4 - dx, dy), CAP)
                arrived(xg.at[g, src, :], d_send.at[g, i], d_recv.at[g, i])
            send(xg.at[g], xg.at[g], dsib_send.at[g], dsib_recv.at[g], sibling)

        def sib_x(g):
            arrived(xg.at[g], dsib_send.at[g], dsib_recv.at[g])

        def exchange_y():
            for i, (dx, dy) in enumerate(partners):
                j = group_of(dx, dy)
                send(
                    send_y.at[rows_of(j, CAP), :], yd.at[z, own_rows, :],
                    a_send.at[i], a_recv.at[i], dev(j, yh, z, core),
                )

        def y_arrived():
            for i, (dx, dy) in enumerate(partners):
                src = rows_of(group_of(4 - dx, dy), CAP)
                arrived(yd.at[z, src, :], a_send.at[i], a_recv.at[i])

        def sib_y(*ds):
            for d in ds:
                for p in range(NP):
                    arrived(yd_view(zmod(z + d), p), sib_send.at[d % NZ, p], sib_recv.at[d % NZ, p])

        def gather():
            for s in range(5):
                for p in range(NP):
                    for way, nxt, sign in ((0, up, -1), (1, down, 1)):
                        split = (p < NP // 2) == (way == 0)
                        if s == 4 and not split:
                            continue
                        ref = yd_view(zmod(z + sign * s), p)
                        if s > 0:
                            arrived(ref, ring_send.at[way, s - 1, p], ring_recv.at[way, s - 1, p])
                        if s < 3 or (s == 3 and split):
                            send(ref, ref, ring_send.at[way, s, p], ring_recv.at[way, s, p], nxt)
                        if s > 0 or way == 0:
                            d = (sign * s) % NZ
                            send(ref, ref, sib_send.at[d, p], sib_recv.at[d, p], sibling)
                yield

        def spread_out(view, sems):
            s_send, s_recv, b_send, b_recv = sems

            def at(dz):
                return dev(e, yh, zmod(z + dz), core)

            def pass_on(d, h=None):
                ref = view(t, zmod(z + d), h)
                k = d % NZ if h != 1 else NZ
                send(ref, ref, b_send.at[k], b_recv.at[k], sibling)

            def got(i, d, h=None):
                arrived(view(t, zmod(z + d), h), s_send.at[i], s_recv.at[i])

            def give(i, d, dz, h=None):
                ref = view(t, zmod(z + d), h)
                send(ref, ref, s_send.at[i], s_recv.at[i], at(dz))

            give(0, 0, 2)
            give(1, 0, -2)
            give(2, 0, 1)
            give(3, 0, -1)
            pass_on(0)
            yield
            got(0, -2)
            give(4, -2, 1)
            give(5, -2, 2, 0)
            got(1, 2)
            give(6, 2, -1)
            give(7, 2, -2, 1)
            pass_on(-2)
            pass_on(2)
            got(2, -1)
            pass_on(-1)
            got(3, 1)
            pass_on(1)
            yield
            got(4, -3)
            pass_on(-3)
            got(6, 3)
            pass_on(3)
            got(5, -4, 0)
            pass_on(4, 0)
            got(7, 4, 1)
            pass_on(4, 1)
            yield

        def term(zd):
            cols = rows_of(zd, RS)
            if t == 0:
                v = jnp.dot(hid[...], wd[:, cols], preferred_element_type=F32)
            else:
                v = lax.dot_general(gpre[...], wgu[cols, :], NT, preferred_element_type=F32)
            for q in range(NQ):
                part[q, zd] = v[:, q * QC : (q + 1) * QC].astype(BF16)

        def other_terms():
            @pl.loop(0, 5)
            def _(i):
                term(zmod(z + 6 + i))

        probs = []

        def back(q):
            shared = q == NQ - 1

            def half(h):
                if shared:
                    return pl.ds(pl.multiple_of(yh * HALF + h * (HALF // 2), HALF // 2), HALF // 2)
                return slice(h * HALF, (h + 1) * HALF)

            def add_other(zd, d):
                if shared:
                    mine = rows_of(yh, HALF)
                    arrived(yx.at[zd], yx_send.at[d % NZ], yx_recv.at[d % NZ])
                    part[q, zd, mine, :] = (part[q, zd, mine, :].astype(F32) + yx[zd].astype(F32)).astype(BF16)

            def rs_start(way, s, h):
                send(
                    part.at[q, target(way, s), half(h), :], land[way].at[q, s, half(h), :],
                    rs_send.at[q, way * 4 + s, h], rs_recv.at[q, way * 4 + s, h], up if way == 0 else down,
                )

            def rs_arrived(way, s, h):
                arrived(land[way].at[q, s, half(h), :], rs_send.at[q, way * 4 + s, h], rs_recv.at[q, way * 4 + s, h])

            def rs_add(way, s, h):
                zd = target(way, s + 1)
                part[q, zd, half(h), :] = (
                    part[q, zd, half(h), :].astype(F32) + land[way][q, s, half(h), :].astype(F32)
                ).astype(BF16)

            if shared:
                for d in (4, 3, 5, 2, 6, 1, 7, 0):
                    zd = zmod(z + d)
                    send(
                        part.at[q, zd, rows_of(1 - yh, HALF), :], yx.at[zd],
                        yx_send.at[d], yx_recv.at[d], dev(e, 1 - yh, z, core),
                    )
                yield
            if q == 0:
                term(zmod(z + 4))
            add_other(zmod(z + 4), 4)
            rs_start(0, 0, 0)
            rs_start(1, 0, 1)
            if q == 0:
                term(zmod(z + 3))
            add_other(zmod(z + 3), 3)
            rs_start(0, 1, 1)
            if q == 0:
                term(zmod(z + 5))
            add_other(zmod(z + 5), 5)
            rs_start(1, 1, 0)
            yield
            for way, h in ((0, 0), (1, 1)):
                rs_arrived(way, 0, h)
                rs_add(way, 0, h)
                rs_start(way, 1, h)
            yield
            for s in (1, 2):
                add_other(zmod(z + 3 - s), 3 - s)
                add_other(zmod(z + 5 + s), 5 + s)
                for way, h in ((0, 1), (1, 0), (0, 0), (1, 1)):
                    rs_arrived(way, s, h)
                    rs_add(way, s, h)
                    rs_start(way, s + 1, h)
                yield
            add_other(z, 0)
            for h in range(2):
                for way in range(2):
                    rs_arrived(way, 3, h)
                part[q, z, half(h), :] = (
                    part[q, z, half(h), :].astype(F32)
                    + rp[q, 3, half(h), :].astype(F32)
                    + rm[q, 3, half(h), :].astype(F32)
                ).astype(BF16)
            if shared:
                def give(i, dy):
                    b = yh * 4 + lax.rem(ex + i, 4)
                    return remote(
                        part.at[q, z, rows_of(b, CAP), :], rc.at[q, 0, own_rows, :],
                        c_send.at[q, i * 2 + dy], c_recv.at[q, i * 2 + ey], dev(b, lax.rem(yh + dy, 2), z, core),
                    )

                @pl.when(yh == ey)
                def _():
                    rc[q, 0, own_rows, :] = part[q, z, own_rows, :]

                @pl.when(yh != ey)
                def _():
                    give(0, 0).start()

                for i in range(4):
                    for dy in range(2):
                        if i or dy:
                            c = give(i, dy)
                            c.start()
                            pending.append(c)
            else:
                rc[q, yh, own_rows, :] = part[q, z, own_rows, :]
                for i in range(E):
                    for dy in range(2):
                        if i or dy:
                            b = lax.rem(e + i, E)
                            send(
                                part.at[q, z, rows_of(b, CAP), :], rc.at[q, yh, own_rows, :],
                                c_send.at[q, i * 2 + dy], c_recv.at[q, i * 2 + dy],
                                dev(b, lax.rem(yh + dy, 2), z, core),
                            )
            yield
            if shared:
                for i in range(4):
                    for side in range(2):
                        src = rc.at[q, 0, rows_of(side * 4 + lax.rem(ex + 4 - i, 4), CAP), :]
                        if i:
                            arrived(src, c_send.at[q, i * 2 + side], c_recv.at[q, i * 2 + side])
                        else:

                            @pl.when(jnp.logical_or(yh != ey, ey != side))
                            def _(src=src, side=side):
                                arrived(src, c_send.at[q, side], c_recv.at[q, side])

                @pl.when(yh != ey)
                def _():
                    give(0, 0).wait_send()

                summed = rc[q, 0]
            else:
                for i in range(E):
                    for dy in range(2):
                        if i or dy:
                            src = rows_of(lax.rem(e + E - i, E), CAP)
                            arrived(
                                rc.at[q, lax.rem(yh + dy, 2), src, :],
                                c_send.at[q, i * 2 + dy], c_recv.at[q, i * 2 + dy],
                            )
                summed = (rc[q, 0].astype(F32) + rc[q, 1].astype(F32)).astype(BF16)
            out0 = jnp.dot(pick0, summed, preferred_element_type=F32)
            out1 = jnp.dot(pick1, summed, preferred_element_type=F32)
            mixed = w0 * out0 + w1 * out1 if t == 0 else out0 + out1
            outs[t, :, pl.ds(pl.multiple_of(z * RS + q * QC, QC), QC)] = mixed.astype(BF16)

            def columns(zz):
                return pl.ds(pl.multiple_of(zz * RS + q * QC, QC), QC)

            def view(kind, zz, h=None):
                rows = slice(0, TOK) if h is None else slice(h * (TOK // 2), (h + 1) * (TOK // 2))
                return outs.at[kind, rows, columns(zz)]

            sems = (o_send.at[q], o_recv.at[q], osib_send.at[q], osib_recv.at[q])
            steps = spread_out(view, sems)
            next(steps)
            if t == 0:
                cot = cot_part[:, q * QC : (q + 1) * QC].astype(F32)
                probs.append((jnp.sum(cot * out0, axis=1, keepdims=True), jnp.sum(cot * out1, axis=1, keepdims=True)))
                if q == NQ - 1:
                    p0 = sum(v[0] for v in probs)
                    p1 = sum(v[1] for v in probs)
                    gp[z] = (jnp.where(lane == 0, p0, 0.0) + jnp.where(lane == 1, p1, 0.0)).T[0:8, :]
                    for dz in range(1, NZ):
                        send(gp.at[z], gp.at[z], g_send.at[dz], g_recv.at[dz], dev(e, yh, lax.rem(z + dz, NZ), core))
            yield
            for _ in steps:
                yield
            for k in range(NZ + 1):
                h = None if k not in (4, NZ) else k // NZ
                arrived(view(1 - t, zmod(z + (4 if k == NZ else k)), h), osib_send.at[q, k], osib_recv.at[q, k])
            yield

        if t == 0:
            load_x[0].wait()
            send_x[0] = dispatch(acts[0])
        else:
            own_c.wait()
            send_y[...] = dispatch(cot_part[...])
            yd[z, own_rows, :] = send_y[own_rows, :]
        pl.semaphore_wait(barrier, 2 * E - 1 + NZ)
        if t == 0:
            for g in range(NG):
                if g:
                    load_x[g].wait()
                exchange_x(g)
            send(w_gate.at[0], wgu.at[:, 0:H], wpre_sem.at[0], wpre_sem.at[2], sibling)
            send(w_up.at[0], wgu.at[:, 2 * H : 3 * H], wpre_sem.at[1], wpre_sem.at[3], sibling)
        else:
            exchange_y()
            send(w_down.at[0], wd.at[H : 2 * H, :], wpre_sem.at[0], wpre_sem.at[2], sibling)
        acc_gu[...] = jnp.zeros_like(acc_gu)
        acc_h[...] = jnp.zeros_like(acc_h)
        pick0 = spread0.T.astype(BF16)
        pick1 = spread1.T.astype(BF16)
        if t == 0:
            w0 = jnp.broadcast_to(w0_row, (TOK, TOK)).T[:, 0:1]
            w1 = jnp.broadcast_to(w1_row, (TOK, TOK)).T[:, 0:1]
            own_c.wait()
        for c in (own_g, own_u, own_d):
            c.wait()
        ring = gather()
        q0, q1, q2 = (back(q) for q in range(NQ))

        def go(*order):
            for q in order:
                next(q)

        if t == 0:
            x_arrived(0)
            add_x(0)
            sib_y(0)
            add_y(z)
            x_arrived(1)
            add_x(1)
            sib_y(1, -1)
            add_pair(1)
            x_arrived(2)
            add_x(2)
            sib_y(2, -2)
            add_pair(2)
            x_arrived(3)
            add_x(3)
            forward()
            sib_y(3, -3)
            add_pair(3)
            sib_y(4)
            add_y(zmod(z + 4))
            backward()
            send(gpre.at[:, 0:H], gpre.at[:, 0:H], act_sem.at[0], act_sem.at[2], sibling)
            send(gpre.at[:, 2 * H : 3 * H], gpre.at[:, 2 * H : 3 * H], act_sem.at[1], act_sem.at[3], sibling)
            arrived(wd.at[H : 2 * H, :], wpre_sem.at[0], wpre_sem.at[2])
            arrived(hid.at[:, H : 2 * H], act_sem.at[0], act_sem.at[2])
        else:
            y_arrived()
            go(ring)
            add_y(z)
            go(ring)
            add_pair(1)
            sib_x(0)
            add_x(0)
            go(ring)
            add_pair(2)
            sib_x(1)
            add_x(1)
            go(ring)
            add_pair(3)
            sib_x(2)
            add_x(2)
            go(ring)
            add_y(zmod(z + 4))
            sib_x(3)
            add_x(3)
            forward()
            send(hid.at[:, H : 2 * H], hid.at[:, H : 2 * H], act_sem.at[0], act_sem.at[2], sibling)
            backward()
            arrived(wgu.at[:, 0:H], wpre_sem.at[0], wpre_sem.at[2])
            arrived(wgu.at[:, 2 * H : 3 * H], wpre_sem.at[1], wpre_sem.at[3])
            arrived(gpre.at[:, 0:H], act_sem.at[0], act_sem.at[2])
            arrived(gpre.at[:, 2 * H : 3 * H], act_sem.at[1], act_sem.at[3])
        go(q0, q1)
        other_terms()
        go(q2, q0, q1)
        weight_grads(0)
        go(q0, q1, q2)
        weight_grads(1)
        go(q0, q1, q2, q0, q2, q1, q2, q0, q2, q1)
        weight_grads(2)
        go(q0, q2, q1)
        weight_grads(3)
        go(q2, q0, q1)
        if t == 0:
            for dz in range(1, NZ):
                arrived(gp.at[zmod(z - dz)], g_send.at[dz], g_recv.at[dz])
            total = gp[0]
            for zz in range(1, NZ):
                total = total + gp[zz]
            gp_sum[...] = total
            send(gp_sum, gp_sum, gsum_sem.at[0], gsum_sem.at[1], sibling)
        go(q2)
        if t == 1:
            arrived(gp_sum, gsum_sem.at[0], gsum_sem.at[1])
        go(q0, q1, q2)

        for q in (ring, q0, q1, q2):
            assert (t == 0 and q is ring) or next(q, None) is None
        prob[...] = gp_sum[0:2, :]
        for c in pending:
            c.wait_send()

    for c in range(2):

        @pl.when(core == c)
        def _(c=c):
            program(c)


def store(outs, prob, gg, gu, gd, moe_out, grad_tokens, grad_prob, grad_gate, grad_up, grad_down, sem):
    copies = []
    for i, (src, dst) in enumerate((
        (gg, grad_gate.at[0]), (gu, grad_up.at[0]), (gd, grad_down.at[0]),
        (outs.at[0], moe_out), (outs.at[1], grad_tokens), (prob, grad_prob),
    )):
        copies.append(pltpu.make_async_copy(src, dst, sem.at[i]))
    for c in copies:
        c.start()
    for c in copies:
        c.wait()


def per_device(tokens, assignment, route_weight, cotangent, w_gate, w_up, w_down):
    hbm = pl.BlockSpec(memory_space=pl.ANY)
    vmem = pl.BlockSpec(memory_space=pltpu.VMEM)
    dma = pltpu.SemaphoreType.DMA
    held = pl.pallas_call(
        kernel,
        out_shape=(
            pltpu.VMEM((2, TOK, D), BF16),
            pltpu.VMEM((2, TOK), F32),
            pltpu.VMEM((D, H), BF16),
            pltpu.VMEM((D, H), BF16),
            pltpu.VMEM((H, D), BF16),
        ),
        in_specs=[hbm, vmem, vmem, hbm, hbm, hbm, hbm],
        out_specs=(vmem,) * 5,
        scratch_shapes=[
            pltpu.VMEM((NG, TOK, KG), BF16),
            pltpu.VMEM((TOK, RS), BF16),
            pltpu.VMEM((D, 4 * H), BF16),
            pltpu.VMEM((2 * H, D), BF16),
            pltpu.VMEM((NG, SLOTS, KG), BF16),
            pltpu.VMEM((SLOTS, RS), BF16),
            pltpu.VMEM((NG, SLOTS, KG), BF16),
            pltpu.VMEM((NZ, SLOTS, RS), BF16),
            pltpu.VMEM((SLOTS, 2 * H), F32),
            pltpu.VMEM((SLOTS, H), F32),
            pltpu.VMEM((SLOTS, 2 * H), BF16),
            pltpu.VMEM((SLOTS, 4 * H), BF16),
            pltpu.VMEM((NQ, NZ, SLOTS, QC), BF16),
            pltpu.VMEM((NQ, 4, SLOTS, QC), BF16),
            pltpu.VMEM((NQ, 4, SLOTS, QC), BF16),
            pltpu.VMEM((NQ, 2, SLOTS, QC), BF16),
            pltpu.VMEM((NZ, HALF, QC), BF16),
            pltpu.VMEM((NZ, 8, TOK), F32),
            pltpu.VMEM((8, TOK), F32),
            dma((5 + NG,)), dma((4,)),
            dma((E - 1,)), dma((E - 1,)), dma((NG, E - 1)), dma((NG, E - 1)),
            dma((2, 4, NP)), dma((2, 4, NP)), dma((NZ, NP)), dma((NZ, NP)), dma((NG,)), dma((NG,)),
            dma((4,)), dma((NZ,)), dma((NZ,)), dma((NQ, 8, 2)), dma((NQ, 8, 2)), dma((NQ, 2 * E)), dma((NQ, 2 * E)),
            dma((NQ, 8)), dma((NQ, 8)), dma((NQ, NZ + 1)), dma((NQ, NZ + 1)),
            dma((NZ,)), dma((NZ,)), dma((2,)),
        ],
        compiler_params=pltpu.CompilerParams(
            collective_id=0, has_side_effects=True, vmem_limit_bytes=50 * 1024 * 1024
        ),
    )(tokens, assignment.T, route_weight.T, cotangent, w_gate, w_up, w_down)
    moe_out, grad_tokens, grad_prob, grad_gate, grad_up, grad_down = pl.pallas_call(
        store,
        out_shape=(
            jax.ShapeDtypeStruct((TOK, D), BF16),
            jax.ShapeDtypeStruct((TOK, D), BF16),
            jax.ShapeDtypeStruct((2, TOK), F32),
            jax.ShapeDtypeStruct((1, D, H), BF16),
            jax.ShapeDtypeStruct((1, D, H), BF16),
            jax.ShapeDtypeStruct((1, H, D), BF16),
        ),
        in_specs=[vmem] * 5,
        out_specs=(hbm,) * 6,
        scratch_shapes=[dma((6,))],
        compiler_params=pltpu.CompilerParams(vmem_limit_bytes=16 * 1024 * 1024),
    )(*held)
    return (moe_out, grad_tokens, grad_prob.T, grad_gate, grad_up, grad_down)


def solution(mesh):
    return jax.shard_map(
        per_device,
        mesh=mesh,
        in_specs=(
            P("expert", None),
            P("expert", None),
            P("expert", None),
            P("expert", None),
            P("expert", None, "fsdp"),
            P("expert", None, "fsdp"),
            P("expert", "fsdp", None),
        ),
        out_specs=(
            P("expert", None),
            P("expert", None),
            P("expert", None),
            P("expert", None, "fsdp"),
            P("expert", None, "fsdp"),
            P("expert", "fsdp", None),
        ),
        check_vma=False,
    )
```
